256 devices in a mesh: replica: 32 (over z, y), tensor: 2 (over core), section: 4 (over x).
Axes of the slice: x: 4, y: 4, z: 8, core: 2. Of those that a mesh axis runs over, the one named last changes fastest.
Arguments:
- weight: bfloat16 [4096, 1024], P('section', 'tensor'), may hold values from -3 to 3
- grads: bfloat16 [32, 4096, 1024], P('replica', 'section', 'tensor'), may hold values from -83 to 83
- error: bfloat16 [32, 4096, 1024], P('replica', 'section', 'tensor'), may hold values from -3 to 3
- momentum: float32 [4096, 1024], P('section', 'tensor'), may hold values from -6 to 6
- basis: float32 [1024, 32], P('tensor'), may hold values from -6 to 6
- gram_root: float32 [32, 32], replicated, may hold values from -1 to 1
- gain: float32 [2, 4096], P(None, ('tensor', 'section')), may hold values from 0.5 to 1.5
- gain_momentum: float32 [2, 4096], P(None, ('tensor', 'section')), may hold values from -3 to 3
- gain_grads: float32 [32, 2, 4096], P('replica', None, ('tensor', 'section')), may hold values from -176 to 176
Outputs:
- new_weight: bfloat16 [4096, 1024], P(None, 'tensor')
- new_error: bfloat16 [32, 4096, 1024], P('replica', 'section', 'tensor')
- new_momentum: float32 [4096, 1024], P('section', 'tensor')
- new_gain: float32 [2, 4096], replicated
- new_gain_momentum: float32 [2, 4096], P(None, ('tensor', 'section'))
The draws below stay inside these ranges and needn't reach their ends.
All inputs are finite; a program needn't handle non-finite values.
Results may differ from the reference program's by a relative error of at most 0.0004.
Values may be sent and summed in bfloat16 or wider, within the bound.
A program may use at most 64 MiB of HBM per device.

```python
import math
import jax
import jax.numpy as jnp
from jax import lax

D = 4096
KV = 1024
RANK = 32
N_REPLICA = 32


def draw_grads(key, part):
    keys = jax.random.split(jax.random.fold_in(key, 11), 4)
    rise_rows = 1.0 + 2.0 * jnp.arange(D, dtype=jnp.float32) / max(D - 1, 1)
    rise_cols = 1.0 + 2.0 * jnp.arange(KV, dtype=jnp.float32) / max(KV - 1, 1)
    rise_reps = 1.0 + 2.0 * jnp.arange(N_REPLICA, dtype=jnp.float32) / max(N_REPLICA - 1, 1)
    row_scale = jnp.exp(jax.random.uniform(keys[0], (D,), jnp.float32, 0.0, math.log(10.0))) * rise_rows
    col_scale = jnp.exp(jax.random.uniform(keys[1], (KV,), jnp.float32, 0.0, math.log(10.0))) * rise_cols
    own = jnp.clip(jax.random.normal(keys[3], (N_REPLICA, D, KV), jnp.float32), -6.0, 6.0)
    common = jnp.clip(jax.random.normal(keys[2], (D, KV), jnp.float32), -6.0, 6.0)
    mixed = 0.3 * common + own
    values = mixed * row_scale[None, :, None] * col_scale[None, None, :] * rise_reps[:, None, None] / 256.0
    return values.astype(jnp.bfloat16)


def draw_gram_root(key, part):
    keys = jax.random.split(jax.random.fold_in(key, 23), 2)
    diag = 2.0 * jnp.exp(jax.random.uniform(keys[0], (RANK,), jnp.float32, 0.0, math.log(2.0)))
    noise = jnp.clip(jax.random.normal(keys[1], (RANK, RANK), jnp.float32), -4.0, 4.0)
    sym = (noise + noise.T) * (0.5 / math.sqrt(RANK))
    whole = sym + jnp.eye(RANK, dtype=jnp.float32) * diag[:, None]
    return (whole / (2.0 * math.sqrt(D * KV))).astype(jnp.float32)


def draw_gain_grads(key, part):
    keys = jax.random.split(jax.random.fold_in(key, 37), 3)
    rise_cols = 1.0 + 2.0 * jnp.arange(D, dtype=jnp.float32) / max(D - 1, 1)
    rise_reps = 1.0 + 2.0 * jnp.arange(N_REPLICA, dtype=jnp.float32) / max(N_REPLICA - 1, 1)
    col_scale = jnp.exp(jax.random.uniform(keys[0], (2, D), jnp.float32, 0.0, math.log(10.0))) * rise_cols[None]
    own = jnp.clip(jax.random.normal(keys[2], (N_REPLICA, 2, D), jnp.float32), -6.0, 6.0)
    common = jnp.clip(jax.random.normal(keys[1], (2, D), jnp.float32), -6.0, 6.0)
    mixed = 0.3 * common + own
    return (mixed * col_scale[None] * rise_reps[:, None, None] / 4.0).astype(jnp.float32)


def levels(key, dims, pieces, least, high):
    def one(position, blocks):
        draws = jax.random.uniform(jax.random.fold_in(jax.random.fold_in(key, 6), position), (blocks,), jnp.float32, least / len(pieces), high / len(pieces))
        return jnp.repeat(jnp.exp(draws), dims[position] // blocks).reshape((-1,) + (1,) * (len(dims) - position - 1))

    level = one(*pieces[0])
    for cut in pieces[1:]:
        level = level * one(*cut)
    return level


def gaussian(key, dims, spread, bound, cuts=(), kind=jnp.bfloat16):
    result = spread * jax.random.normal(key, dims, jnp.float32)
    if cuts:
        result = result * levels(key, dims, cuts, -0.22, 0.18)
    return jnp.clip(result, -bound, bound).astype(kind)


def setup_inputs(seed: int = 0) -> dict:
    key_list = jax.random.split(jax.random.key(seed), 10)
    return {
        "weight": gaussian(key_list[0], (D, KV), 0.5, 3.0, ((0, 4), (1, 2))),
        "grads": draw_grads(jax.random.fold_in(key_list[9], 71), 0),
        "error": gaussian(key_list[2], (N_REPLICA, D, KV), 0.5, 3.0, ((0, 32), (1, 4), (2, 2))),
        "momentum": gaussian(key_list[3], (D, KV), 1.0, 6.0, ((0, 4), (1, 2)), jnp.float32),
        "basis": gaussian(key_list[4], (KV, RANK), 1.0, 6.0, ((0, 2),), jnp.float32),
        "gram_root": draw_gram_root(jax.random.fold_in(key_list[9], 71), 0),
        "gain": jnp.clip(1.0 + 0.1 * jax.random.normal(key_list[6], (2, D), jnp.float32), 0.5, 1.5),
        "gain_momentum": gaussian(key_list[7], (2, D), 0.5, 3.0, ((1, 8),), jnp.float32),
        "gain_grads": draw_gain_grads(jax.random.fold_in(key_list[9], 71), 0),
    }


def reference(weight, grads, error, momentum, basis, gram_root, gain, gain_momentum, gain_grads):
    highest = lax.Precision.HIGHEST

    def left_term(total, pair):
        merged = pair[0].astype(jnp.float32) + pair[1].astype(jnp.float32)
        return (total + jnp.dot(merged, basis, precision=highest), None)
    lowp_total, unused = lax.scan(left_term, jnp.zeros((D, RANK), jnp.float32), (grads, error))
    lowp = lowp_total / N_REPLICA
    ortho = jnp.dot(lowp, gram_root, precision=highest)

    def right_term(total, pair):
        merged = pair[0].astype(jnp.float32) + pair[1].astype(jnp.float32)
        return (total + jnp.dot(merged.T, ortho, precision=highest), None)
    basis_total, unused = lax.scan(right_term, jnp.zeros((KV, RANK), jnp.float32), (grads, error))
    newbasis = basis_total / N_REPLICA
    approx = jnp.dot(ortho, newbasis.T, precision=highest)
    merged_all = grads.astype(jnp.float32) + error.astype(jnp.float32)
    new_error = (merged_all - approx[None]).astype(jnp.bfloat16)
    scale = lax.rsqrt(jnp.mean(approx * approx) + 1e-06)
    update = scale * approx
    new_momentum = 0.9 * momentum + update
    new_weight = (weight.astype(jnp.float32) - 0.05 * (update + 0.9 * new_momentum)).astype(jnp.bfloat16)
    gain_mean = lax.optimization_barrier(jnp.sum(gain_grads, axis=0)) / N_REPLICA
    new_gain_momentum = 0.9 * gain_momentum + gain_mean
    new_gain = gain - 0.02 * (gain_mean + 0.9 * new_gain_momentum)
    return (new_weight, new_error, new_momentum, new_gain, new_gain_momentum)
```

```python
import functools

import jax
import jax.numpy as jnp
from jax import lax
from jax.experimental import pallas as pl
from jax.experimental.pallas import tpu as pltpu
from jax.sharding import PartitionSpec as P

MESH = pl.DeviceIdType.MESH
F32 = jnp.float32
BF16 = jnp.bfloat16
HIGHEST = lax.Precision.HIGHEST
NY = 4
LANES = 128
SUB = 8


def split3(value):
    first = value.astype(BF16)
    rest = value - first.astype(F32)
    second = rest.astype(BF16)
    third = (rest - second.astype(F32)).astype(BF16)
    return first, second, third


def dot(left, right, dims):
    return lax.dot_general(left, right, (dims, ((), ())), preferred_element_type=F32)


def exchange_kernel(
    sizes,
    basis_ref, gram_ref, gaing_ref, gain_ref, gainm_ref,
    grads_ref, error_ref, weight_ref, momentum_ref,
    scale_out, nb_out, ortho_out, gains_out, gainm_out, moved_ref,
    g_buf, e_buf, w_buf, m_buf, c_buf,
    pieces, opieces, left_send, left_recv, mid_send, mid_recv, ortho, right_send, right_recv,
    rmid, newb, gains, pair_send, pair_recv,
    load_sem, ls_sem, lr_sem, ms_sem, mr_sem, os_sem, or_sem, xs_sem, xr_sem,
    rs_sem, rr_sem, ns_sem, nr_sem, as_sem, ar_sem, bs_sem, br_sem, gs_sem, gr_sem, ps_sem, pr_sem,
):
    nz, nt, nx, rank = sizes
    replicas = nz * NY
    rep = lax.axis_index("replica")
    core = lax.axis_index("tensor")
    x = lax.axis_index("section")
    z = rep // NY
    y = rep % NY
    rows, cols = c_buf.shape
    nc = nt * NY
    nxy = nx * NY
    steps = rows // nc

    loads = []
    for position, (source, target) in enumerate(
        ((grads_ref.at[0], g_buf), (error_ref.at[0], e_buf), (weight_ref, w_buf), (momentum_ref, m_buf))
    ):
        load = pltpu.make_async_copy(source, target, load_sem.at[position])
        load.start()
        loads.append(load)

    def spot(dz=0, dy=0, dc=0, dx=0):
        there = (lax.rem(z + dz, nz) * NY + lax.rem(y + dy, NY), lax.rem(core + dc, nt), lax.rem(x + dx, nx))
        return there

    cy_peers = [(dc, dy) for dc in range(nt) for dy in range(NY) if (dc, dy) != (0, 0)]
    xy_peers = [(dx, dy) for dx in range(nx) for dy in range(NY) if (dx, dy) != (0, 0)]
    cy_peers.sort(key=lambda p: (-min(p[1], NY - p[1]), -p[0]))
    xy_peers.sort(key=lambda p: -min(p[1], NY - p[1]) - min(p[0], nx - p[0]))
    z_peers = sorted(range(1, nz), key=lambda d: -min(d, nz - d))
    greet = {(0, dy, dc, 0) for dc, dy in cy_peers} | {(0, dy, 0, dx) for dx, dy in xy_peers}
    greet |= {(dz, 0, 0, 0) for dz in z_peers}
    greet = sorted(greet)

    barrier = pltpu.get_barrier_semaphore()
    for dz, dy, dc, dx in greet:
        pl.semaphore_signal(barrier, inc=1, device_id=spot(dz, dy, dc, dx), device_id_type=MESH)

    def send(source, target, ssem, rsem, there):
        copy = pltpu.make_async_remote_copy(
            src_ref=source, dst_ref=target, send_sem=ssem, recv_sem=rsem, device_id=there, device_id_type=MESH
        )
        copy.start()
        return copy

    def arrive(target, ssem, rsem, there):
        pltpu.make_async_remote_copy(
            src_ref=target, dst_ref=target, send_sem=ssem, recv_sem=rsem, device_id=there, device_id_type=MESH
        ).wait_recv()

    sent = []
    mine = core * NY + y

    b1, b2, b3 = split3(basis_ref[...])
    pieces[0:rank, :] = b1
    pieces[rank : 2 * rank, :] = b2
    pieces[2 * rank : 3 * rank, :] = b3
    loads[0].wait()
    loads[1].wait()
    low = dot(pieces[...], g_buf[...], ((1,), (1,))) + dot(pieces[...], e_buf[...], ((1,), (1,)))
    low = low[0:rank] + low[rank : 2 * rank] + low[2 * rank : 3 * rank]
    for k in range(nc):
        left_send[k, 0:rank, :] = low[:, k * steps : (k + 1) * steps]
        own = jnp.where(core == k // NY, 1.0, 0.0).astype(F32)
        for i in range(2):
            for j in range(4):
                row = rank + i * 4 + j
                left_send[k, row : row + 1, :] = gaing_ref[0, i : i + 1, j * LANES : (j + 1) * LANES] * own

    pl.semaphore_wait(barrier, len(greet))

    for slot, (dc, dy) in enumerate(cy_peers):
        there = spot(dy=dy, dc=dc)
        sent.append(
            send(left_send.at[there[1] * NY + lax.rem(y + dy, NY)], left_recv.at[slot], ls_sem.at[slot], lr_sem.at[slot], there)
        )

    loads[2].wait()
    loads[3].wait()
    c_buf[...] = w_buf[...].astype(F32) - 0.0405 * m_buf[...]
    keep = pltpu.make_async_copy(c_buf, moved_ref.at[x], load_sem.at[4])
    keep.start()
    for slot, dx in enumerate((2, 1, 3)):
        sent.append(send(c_buf, moved_ref.at[x], bs_sem.at[slot], br_sem.at[slot], spot(dx=dx)))

    total = left_send[mine]
    for slot in range(len(cy_peers)):
        sent[slot].wait_recv()
        total = total + left_recv[slot]
    mid_recv[z] = total
    for slot, dz in enumerate(z_peers):
        sent.append(send(mid_recv.at[z], mid_recv.at[z], ms_sem.at[slot], mr_sem.at[z], spot(dz=dz)))
    for slot, dz in enumerate(z_peers):
        there = lax.rem(z + dz, nz)
        arrive(mid_recv.at[there], ms_sem.at[slot], mr_sem.at[there], spot(dz=dz))
    total = mid_recv[0]
    for k in range(1, nz):
        total = total + mid_recv[k]
    total = total * (1.0 / replicas)
    ortho[x, mine] = lax.dot_general(
        gram_ref[...], total[0:rank], (((0,), (0,)), ((), ())), precision=HIGHEST, preferred_element_type=F32
    )
    for slot, (dc, dy) in enumerate(cy_peers):
        sent.append(send(ortho.at[x, mine], ortho.at[x, mine], os_sem.at[slot], or_sem.at[mine], spot(dy=dy, dc=dc)))
    mean = total[rank : rank + 8]
    new_gainm = 0.9 * gainm_ref[...] + mean
    gainm_out[...] = new_gainm
    group = core * nx + x
    gains[group] = gain_ref[...] - 0.02 * (mean + 0.9 * new_gainm)
    for slot, dx in enumerate((2, 1, 3)):
        sent.append(send(gains.at[group], gains.at[group], gs_sem.at[slot], gr_sem.at[x], spot(dx=dx)))
    for slot, (dc, dy) in enumerate(cy_peers):
        there = spot(dy=dy, dc=dc)
        index = there[1] * NY + lax.rem(y + dy, NY)
        arrive(ortho.at[x, index], os_sem.at[slot], or_sem.at[index], there)

    for slot, dx in enumerate((2, 1, 3)):
        sent.append(send(ortho.at[x], ortho.at[x], xs_sem.at[slot], xr_sem.at[x], spot(dx=dx)))
    for k in range(nc):
        parts = split3(ortho[x, k])
        for p in range(3):
            opieces[p * rank : (p + 1) * rank, k * steps : (k + 1) * steps] = parts[p]
    right = dot(opieces[...], g_buf[...], ((1,), (0,))) + dot(opieces[...], e_buf[...], ((1,), (0,)))
    right = right[0:rank] + right[rank : 2 * rank] + right[2 * rank : 3 * rank]
    across = cols // LANES
    for i in range(rank // SUB):
        for j in range(across):
            right_send[i * across + j] = right[i * SUB : (i + 1) * SUB, j * LANES : (j + 1) * LANES]

    place = x * NY + y
    started = len(sent)
    for slot, (dx, dy) in enumerate(xy_peers):
        there = spot(dy=dy, dx=dx)
        sent.append(
            send(right_send.at[there[2] * NY + lax.rem(y + dy, NY)], right_recv.at[slot], rs_sem.at[slot], rr_sem.at[slot], there)
        )
    total = right_send[place]
    for slot in range(len(xy_peers)):
        sent[started + slot].wait_recv()
        total = total + right_recv[slot]
    rmid[z] = total
    for slot, dz in enumerate(z_peers):
        sent.append(send(rmid.at[z], rmid.at[z], ns_sem.at[slot], nr_sem.at[z], spot(dz=dz)))
    for slot, dz in enumerate(z_peers):
        there = lax.rem(z + dz, nz)
        arrive(rmid.at[there], ns_sem.at[slot], nr_sem.at[there], spot(dz=dz))
    total = rmid[0]
    for k in range(1, nz):
        total = total + rmid[k]
    newb[place] = total * (1.0 / replicas)
    for slot, (dx, dy) in enumerate(xy_peers):
        sent.append(send(newb.at[place], newb.at[place], as_sem.at[slot], ar_sem.at[place], spot(dy=dy, dx=dx)))

    for slot, dx in enumerate((2, 1, 3)):
        there = lax.rem(x + dx, nx)
        arrive(ortho.at[there], xs_sem.at[slot], xr_sem.at[there], spot(dx=dx))
        index = core * nx + there
        arrive(gains.at[index], gs_sem.at[slot], gr_sem.at[there], spot(dx=dx))
    gsq = jnp.zeros((2 * rank, 2 * rank), F32)
    for s in range(nx):
        for k in range(nc):
            parts = split3(ortho[s, k])
            both = jnp.concatenate(parts[0:2], axis=0)
            gsq = gsq + dot(both, both, ((1,), (1,)))
    gsq = gsq[0:rank, 0:rank] + gsq[0:rank, rank:] + gsq[rank:, 0:rank] + gsq[rank:, rank:]

    for slot, (dx, dy) in enumerate(xy_peers):
        there = spot(dy=dy, dx=dx)
        index = there[2] * NY + lax.rem(y + dy, NY)
        arrive(newb.at[index], as_sem.at[slot], ar_sem.at[index], there)

    nsq = jnp.zeros((2 * rank, 2 * rank), F32)
    for j in range(across):
        col = jnp.concatenate([newb[i * across + j] for i in range(rank // SUB)], axis=0)
        parts = split3(col)
        both = jnp.concatenate(parts[0:2], axis=0)
        nsq = nsq + dot(both, both, ((1,), (1,)))
    nsq = nsq[0:rank, 0:rank] + nsq[0:rank, rank:] + nsq[rank:, 0:rank] + nsq[rank:, rank:]
    pair_send[:, 0:rank] = nsq
    other = spot(dc=1)
    pair = send(pair_send, pair_recv, ps_sem.at[0], pr_sem.at[0], other)
    half = pl.ds(core * nx, nx)
    sent.append(send(gains.at[half], gains.at[half], ps_sem.at[1], pr_sem.at[1], other))
    sent.append(pair)

    nb_out[...] = newb[...]
    ortho_out[...] = ortho[...]
    pair.wait_recv()
    square = jnp.sum(gsq * (nsq + pair_recv[:, 0:rank]))
    mean_square = square * (1.0 / (rows * cols * nt * nx))
    scale_out[...] = lax.rsqrt(jnp.full((SUB, LANES), mean_square + 1e-06, F32))
    half = pl.ds(other[1] * nx, nx)
    arrive(gains.at[half], ps_sem.at[1], pr_sem.at[1], other)
    gains_out[...] = gains[...]
    keep.wait()
    for slot, dx in enumerate((2, 1, 3)):
        arrive(moved_ref.at[lax.rem(x + (nx - dx), nx)], bs_sem.at[slot], br_sem.at[slot], spot(dx=dx))
    for copy in sent:
        copy.wait_send()


def apply_kernel(
    sizes, scale_ref, nb_ref, ortho_ref, gains_ref, moved_ref, g_ref, e_ref, m_ref,
    weight_out, error_out, momentum_out, gain_out, right, left,
):
    nz, nt, nx, rank = sizes
    step = pl.program_id(0)
    x = lax.axis_index("section")
    across = nb_ref.shape[0] // (rank // SUB)
    nc = ortho_ref.shape[1]
    order_right = (0, 1, 2, 0, 1, 0)
    order_left = (0, 0, 0, 1, 1, 2)

    @pl.when(step == 0)
    def _():
        for j in range(across):
            col = jnp.concatenate([nb_ref[i * across + j] for i in range(rank // SUB)], axis=0)
            parts = split3(col)
            for p in range(6):
                right[p * rank : (p + 1) * rank, j * LANES : (j + 1) * LANES] = parts[order_right[p]]
        for t in range(nt * nx):
            for i in range(2):
                for j in range(4):
                    at = (t * 4 + j) * LANES
                    gain_out[i : i + 1, at : at + LANES] = gains_ref[t, i * 4 + j : i * 4 + j + 1, :]

    scale = scale_ref[0:1, 0:1]
    size = m_ref.shape[0]
    per = size // LANES

    def product(s):
        for q in range(per):
            parts = split3(ortho_ref[s, step * per + q])
            for p in range(6):
                left[p * rank : (p + 1) * rank, q * LANES : (q + 1) * LANES] = parts[order_left[p]]
        return dot(left[...], right[...], ((0,), (0,)))

    for s in range(nx):
        weight_out[s] = (moved_ref[s] - (0.095 * scale) * product(s)).astype(BF16)
    approx = product(x)
    error_out[0] = (g_ref[0].astype(F32) + e_ref[0].astype(F32) - approx).astype(BF16)
    momentum_out[...] = 0.9 * m_ref[...] + scale * approx


def on_device(weight, grads, error, momentum, basis, gram_root, gain, gain_momentum, gain_grads):
    replicas = lax.axis_size("replica")
    nt = lax.axis_size("tensor")
    nx = lax.axis_size("section")
    rows, cols = weight.shape
    rank = gram_root.shape[0]
    nz = replicas // NY
    sizes = (nz, nt, nx, rank)
    nc = nt * NY
    nxy = nx * NY
    chunk = rows // nc
    vmem = pl.BlockSpec(memory_space=pltpu.VMEM)
    hbm = pl.BlockSpec(memory_space=pl.ANY)
    dma = pltpu.SemaphoreType.DMA
    scale, newb, ortho, gains, gainm, moved = pl.pallas_call(
        functools.partial(exchange_kernel, sizes),
        out_shape=(
            jax.ShapeDtypeStruct((SUB, LANES), F32),
            jax.ShapeDtypeStruct((nxy, SUB, LANES), F32),
            jax.ShapeDtypeStruct((nx, nc, rank, chunk), F32),
            jax.ShapeDtypeStruct((nt * nx, SUB, LANES), F32),
            jax.ShapeDtypeStruct((SUB, LANES), F32),
            jax.ShapeDtypeStruct((nx, rows, cols), F32),
        ),
        in_specs=[vmem] * 5 + [hbm] * 4,
        out_specs=(vmem, vmem, vmem, vmem, vmem, hbm),
        scratch_shapes=[
            pltpu.VMEM((rows, cols), BF16),
            pltpu.VMEM((rows, cols), BF16),
            pltpu.VMEM((rows, cols), BF16),
            pltpu.VMEM((rows, cols), F32),
            pltpu.VMEM((rows, cols), F32),
            pltpu.VMEM((3 * rank, cols), BF16),
            pltpu.VMEM((3 * rank, rows), BF16),
            pltpu.VMEM((nc, rank + SUB, chunk), F32),
            pltpu.VMEM((nc - 1, rank + SUB, chunk), F32),
            pltpu.VMEM((SUB, LANES), F32),
            pltpu.VMEM((nz, rank + SUB, chunk), F32),
            pltpu.VMEM((nx, nc, rank, chunk), F32),
            pltpu.VMEM((nxy, SUB, LANES), F32),
            pltpu.VMEM((nxy - 1, SUB, LANES), F32),
            pltpu.VMEM((nz, SUB, LANES), F32),
            pltpu.VMEM((nxy, SUB, LANES), F32),
            pltpu.VMEM((nt * nx, SUB, LANES), F32),
            pltpu.VMEM((rank, LANES), F32),
            pltpu.VMEM((rank, LANES), F32),
            dma((5,)),
            dma((nc,)), dma((nc,)),
            dma((nz,)), dma((nz,)),
            dma((nc,)), dma((nc,)),
            dma((nx,)), dma((nx,)),
            dma((nxy,)), dma((nxy,)),
            dma((nz,)), dma((nz,)),
            dma((nxy,)), dma((nxy,)),
            dma((nx,)), dma((nx,)),
            dma((nx,)), dma((nx,)),
            dma((2,)), dma((2,)),
        ],
        compiler_params=pltpu.CompilerParams(
            collective_id=0, has_side_effects=True, vmem_limit_bytes=24 * 1024 * 1024
        ),
    )(
        basis.T, gram_root, gain_grads, gain.reshape(SUB, LANES), gain_momentum.reshape(SUB, LANES),
        grads, error, weight, momentum,
    )
    size = 256
    new_weight, new_error, new_momentum, new_gain = pl.pallas_call(
        functools.partial(apply_kernel, sizes),
        grid=(rows // size,),
        out_shape=(
            jax.ShapeDtypeStruct((nx, rows, cols), BF16),
            jax.ShapeDtypeStruct((1, rows, cols), BF16),
            jax.ShapeDtypeStruct((rows, cols), F32),
            jax.ShapeDtypeStruct((2, nt * nx * 4 * LANES), F32),
        ),
        in_specs=[
            vmem, vmem, vmem, vmem,
            pl.BlockSpec((nx, size, cols), lambda i: (0, i, 0)),
            pl.BlockSpec((1, size, cols), lambda i: (0, i, 0)),
            pl.BlockSpec((1, size, cols), lambda i: (0, i, 0)),
            pl.BlockSpec((size, cols), lambda i: (i, 0)),
        ],
        out_specs=(
            pl.BlockSpec((nx, size, cols), lambda i: (0, i, 0)),
            pl.BlockSpec((1, size, cols), lambda i: (0, i, 0)),
            pl.BlockSpec((size, cols), lambda i: (i, 0)),
            vmem,
        ),
        scratch_shapes=[pltpu.VMEM((6 * rank, cols), BF16), pltpu.VMEM((6 * rank, size), BF16)],
        compiler_params=pltpu.CompilerParams(vmem_limit_bytes=24 * 1024 * 1024),
    )(scale, newb, ortho, gains, moved, grads, error, momentum)
    return (
        new_weight.reshape(nx * rows, cols), new_error, new_momentum, new_gain, gainm.reshape(2, 4 * LANES)
    )


def solution(mesh):
    placed = (
        P("section", "tensor"),
        P("replica", "section", "tensor"),
        P("replica", "section", "tensor"),
        P("section", "tensor"),
        P("tensor", None),
        P(),
        P(None, ("tensor", "section")),
        P(None, ("tensor", "section")),
        P("replica", None, ("tensor", "section")),
    )
    return jax.shard_map(
        on_device,
        mesh=mesh,
        in_specs=placed,
        out_specs=(
            P(None, "tensor"),
            P("replica", "section", "tensor"),
            P("section", "tensor"),
            P(),
            P(None, ("tensor", "section")),
        ),
        check_vma=False,
    )
```

```python
import functools

import jax
import jax.numpy as jnp
from jax import lax
from jax.experimental import pallas as pl
from jax.experimental.pallas import tpu as pltpu
from jax.sharding import PartitionSpec as P

MESH = pl.DeviceIdType.MESH
F32 = jnp.float32
BF16 = jnp.bfloat16
HIGHEST = lax.Precision.HIGHEST
NY = 4
LANES = 128
SUB = 8
PIECE = 16
ORDER = ("y++", "y--", "z+-", "z-+") * 3 + ("y++", "y--")
COUNT = len(ORDER)


def ops(text):
    found = []
    for word in text.split():
        name = word.rstrip("0123456789")
        number = word[len(name) :]
        found.append((name, int(number) if number else 0))
    return found


PLAN = (
    ops("x0 x1 x2 x3 x4 x5 x6 x7 x8"),
    ops("a0 a1 a2 a3"),
    ops("b0 b1 a4 a5"),
    ops("x9 x10 x11 x12 x13 b2 b3 a6 a7"),
    ops("b4 b5 a8 a9"),
    ops("X b6 b7 a10 a11"),
    ops("b8 b9 a12 a13"),
    ops("b10 b11 b12 b13") + [("w", j) for j in range(COUNT)] + ops("XW"),
)


def split3(value):
    first = value.astype(BF16)
    rest = value - first.astype(F32)
    second = rest.astype(BF16)
    third = (rest - second.astype(F32)).astype(BF16)
    return first, second, third


def dot(left, right, dims):
    return lax.dot_general(left, right, (dims, ((), ())), preferred_element_type=F32)


def exchange_kernel(
    sizes,
    grads_ref, error_ref, weight_ref, momentum_ref, basis_in, gram_in, gaing_in, gain_in, gainm_in,
    scale_out, nb_out, ortho_out, gains_out, gainm_out, moved_ref,
    g_buf, e_buf, w_buf, m_buf, basis_ref, gram_ref, gaing_ref, gain_ref, gainm_ref, c_buf,
    pieces, opieces, left_send, left_recv, mid_recv, ortho, right_send, right_recv,
    rmid, newb, gains, gain_y, gain_z, pair_send, pair_recv,
    load_sem, ls_sem, lr_sem, ms_sem, mr_sem, os_sem, or_sem, xs_sem, xr_sem,
    rs_sem, rr_sem, ns_sem, nr_sem, as_sem, ar_sem, bs_sem, br_sem, gs_sem, gr_sem, ps_sem, pr_sem,
    gys_sem, gyr_sem, gzs_sem, gzr_sem, qs_sem, qr_sem,
):
    nz, nt, nx, rank = sizes
    replicas = nz * NY
    rep = lax.axis_index("replica")
    core = lax.axis_index("tensor")
    x = lax.axis_index("section")
    z = rep // NY
    y = rep % NY
    rows, cols = c_buf.shape
    nc = nt * NY
    steps = rows // nc

    loads = []
    for position, (source, target) in enumerate(
        (
            (basis_in, basis_ref), (grads_ref.at[0], g_buf), (error_ref.at[0], e_buf), (gaing_in, gaing_ref),
            (weight_ref, w_buf), (momentum_ref, m_buf), (gram_in, gram_ref), (gain_in, gain_ref), (gainm_in, gainm_ref),
        )
    ):
        load = pltpu.make_async_copy(source, target, load_sem.at[position])
        load.start()
        loads.append(load)

    def spot(dz=0, dy=0, dc=0, dx=0):
        return (lax.rem(z + dz, nz) * NY + lax.rem(y + dy, NY), lax.rem(core + dc, nt), lax.rem(x + dx, nx))

    cy_peers = [(dc, dy) for dc in range(nt) for dy in range(NY) if (dc, dy) != (0, 0)]
    xy_peers = [(dx, dy) for dx in range(nx) for dy in range(NY) if (dx, dy) != (0, 0)]
    cy_peers.sort(key=lambda p: (-min(p[1], NY - p[1]), -p[0]))
    xy_peers.sort(key=lambda p: -min(p[1], NY - p[1]) - min(p[0], nx - p[0]))
    z_peers = sorted(range(1, nz), key=lambda d: -min(d, nz - d))
    x_peers = (2, 1, 3)
    y_peers = (2, 1, 3)
    greet = {(0, dy, dc, 0) for dc, dy in cy_peers} | {(0, dy, 0, dx) for dx, dy in xy_peers}
    greet |= {(dz, 0, 0, 0) for dz in z_peers}
    greet = sorted(greet)

    barrier = pltpu.get_barrier_semaphore()
    for dz, dy, dc, dx in greet:
        pl.semaphore_signal(barrier, inc=1, device_id=spot(dz, dy, dc, dx), device_id_type=MESH)

    sent = []

    def send(source, target, ssem, rsem, there):
        copy = pltpu.make_async_remote_copy(
            src_ref=source, dst_ref=target, send_sem=ssem, recv_sem=rsem, device_id=there, device_id_type=MESH
        )
        copy.start()
        sent.append(copy)
        return copy

    def arrive(target, ssem, rsem, there):
        pltpu.make_async_remote_copy(
            src_ref=target, dst_ref=target, send_sem=ssem, recv_sem=rsem, device_id=there, device_id_type=MESH
        ).wait_recv()

    ybit = y % 2
    zbit = z % 2

    def plan(j):
        kind = ORDER[j]
        dy = 1 - 2 * ybit if kind[1] == "+" else 2 * ybit - 1
        dz = 1 - 2 * zbit if kind[2] == "+" else 2 * zbit - 1
        to_y = spot(dy=dy + NY)
        to_z = spot(dz=dz + nz)
        if kind[0] == "y":
            return ybit, zbit, to_y, to_z
        return zbit, ybit, to_z, to_y

    def block(j, start, size):
        return pl.ds(pl.multiple_of(j * 4 * PIECE + start, PIECE), size)

    def bulk(*ops):
        for kind, j in ops:
            if kind == "X":
                tail = pl.ds(len(ORDER) * 4 * PIECE, rows - len(ORDER) * 4 * PIECE)
                for slot, dx in enumerate(x_peers):
                    send(c_buf.at[tail], moved_ref.at[nx - dx, tail], bs_sem.at[slot], br_sem.at[nx - dx - 1], spot(dx=dx))
                continue
            if kind == "XW":
                tail = pl.ds(len(ORDER) * 4 * PIECE, rows - len(ORDER) * 4 * PIECE)
                for slot in range(1, nx):
                    arrive(moved_ref.at[slot, tail], bs_sem.at[slot - 1], br_sem.at[slot - 1], spot(dx=slot))
                continue
            low, high, first, second = plan(j)
            mine = block(j, PIECE * (2 * high + low), PIECE)
            theirs = block(j, PIECE * (2 * high + 1 - low), PIECE)
            both = block(j, 2 * PIECE * high, 2 * PIECE)
            rest = block(j, 2 * PIECE * (1 - high), 2 * PIECE)
            if kind == "x":
                for slot, dx in enumerate(x_peers):
                    send(c_buf.at[mine], moved_ref.at[nx - dx, mine], qs_sem.at[j, slot], qr_sem.at[j, nx - dx - 1], spot(dx=dx))
            if kind == "a":
                for slot in range(1, nx):
                    arrive(moved_ref.at[slot, mine], qs_sem.at[j, slot - 1], qr_sem.at[j, slot - 1], spot(dx=slot))
                send(moved_ref.at[1:nx, mine], moved_ref.at[1:nx, mine], qs_sem.at[j, 3], qr_sem.at[j, 3], first)
            if kind == "b":
                arrive(moved_ref.at[1:nx, theirs], qs_sem.at[j, 3], qr_sem.at[j, 3], first)
                send(moved_ref.at[1:nx, both], moved_ref.at[1:nx, both], qs_sem.at[j, 4], qr_sem.at[j, 4], second)
            if kind == "w":
                arrive(moved_ref.at[1:nx, rest], qs_sem.at[j, 4], qr_sem.at[j, 4], second)

    mine = core * NY + y

    loads[0].wait()
    b1, b2, b3 = split3(basis_ref[...])
    pieces[0:rank, :] = b1
    pieces[rank : 2 * rank, :] = b2
    pieces[2 * rank : 3 * rank, :] = b3
    loads[1].wait()
    loads[2].wait()
    low = dot(pieces[...], g_buf[...], ((1,), (1,))) + dot(pieces[...], e_buf[...], ((1,), (1,)))
    low = low[0:rank] + low[rank : 2 * rank] + low[2 * rank : 3 * rank]
    for k in range(nc):
        left_send[k] = low[:, k * steps : (k + 1) * steps]
    for load in loads[3:]:
        load.wait()
    for i in range(2):
        for j in range(4):
            row = i * 4 + j
            gain_y[y, row : row + 1, :] = gaing_ref[0, i : i + 1, j * LANES : (j + 1) * LANES]
    c_buf[...] = w_buf[...].astype(F32) - 0.0405 * m_buf[...]

    pl.semaphore_wait(barrier, len(greet))

    arrivals = []
    for slot, (dc, dy) in enumerate(cy_peers):
        there = spot(dy=dy, dc=dc)
        arrivals.append(
            send(left_send.at[there[1] * NY + lax.rem(y + dy, NY)], left_recv.at[slot], ls_sem.at[slot], lr_sem.at[slot], there)
        )
    for slot, dy in enumerate(y_peers):
        send(gain_y.at[y], gain_y.at[y], gys_sem.at[slot], gyr_sem.at[y], spot(dy=dy))
    keep = pltpu.make_async_copy(c_buf, moved_ref.at[0], load_sem.at[9])
    keep.start()
    bulk(*PLAN[0])

    total = left_send[mine]
    for slot in range(len(cy_peers)):
        arrivals[slot].wait_recv()
        total = total + left_recv[slot]
    mid_recv[z] = total
    for slot, dz in enumerate(z_peers):
        send(mid_recv.at[z], mid_recv.at[z], ms_sem.at[slot], mr_sem.at[z], spot(dz=dz))
    for slot, dy in enumerate(y_peers):
        there = lax.rem(y + dy, NY)
        arrive(gain_y.at[there], gys_sem.at[slot], gyr_sem.at[there], spot(dy=dy))
    gain_z[z] = ((gain_y[0] + gain_y[1]) + gain_y[2]) + gain_y[3]
    bulk(*PLAN[1])
    for slot, dz in enumerate(z_peers):
        there = lax.rem(z + dz, nz)
        arrive(mid_recv.at[there], ms_sem.at[slot], mr_sem.at[there], spot(dz=dz))
    total = mid_recv[0]
    for k in range(1, nz):
        total = total + mid_recv[k]
    ortho[0, mine] = lax.dot_general(
        gram_ref[...], total * (1.0 / replicas), (((0,), (0,)), ((), ())), precision=HIGHEST, preferred_element_type=F32
    )
    for slot, (dc, dy) in enumerate(cy_peers):
        send(ortho.at[0, mine], ortho.at[0, mine], os_sem.at[slot], or_sem.at[mine], spot(dy=dy, dc=dc))
    for slot, dz in enumerate(z_peers):
        send(gain_z.at[z], gain_z.at[z], gzs_sem.at[slot], gzr_sem.at[z], spot(dz=dz))
    bulk(*PLAN[2])
    for slot, (dc, dy) in enumerate(cy_peers):
        there = spot(dy=dy, dc=dc)
        index = there[1] * NY + lax.rem(y + dy, NY)
        arrive(ortho.at[0, index], os_sem.at[slot], or_sem.at[index], there)

    for k in range(nc):
        parts = split3(ortho[0, k])
        for p in range(3):
            opieces[p * rank : (p + 1) * rank, k * steps : (k + 1) * steps] = parts[p]
    right = dot(opieces[...], g_buf[...], ((1,), (0,))) + dot(opieces[...], e_buf[...], ((1,), (0,)))
    right = right[0:rank] + right[rank : 2 * rank] + right[2 * rank : 3 * rank]
    across = cols // LANES
    for i in range(rank // SUB):
        for j in range(across):
            right_send[i * across + j] = right[i * SUB : (i + 1) * SUB, j * LANES : (j + 1) * LANES]

    place = x * NY + y
    arrivals = []
    for slot, (dx, dy) in enumerate(xy_peers):
        there = spot(dy=dy, dx=dx)
        arrivals.append(
            send(right_send.at[there[2] * NY + lax.rem(y + dy, NY)], right_recv.at[slot], rs_sem.at[slot], rr_sem.at[slot], there)
        )
    half = pl.ds(core * NY, NY)
    for slot, dx in enumerate(x_peers):
        send(ortho.at[0, half], ortho.at[nx - dx, half], xs_sem.at[slot], xr_sem.at[nx - dx - 1], spot(dx=dx))
    for slot, dz in enumerate(z_peers):
        there = lax.rem(z + dz, nz)
        arrive(gain_z.at[there], gzs_sem.at[slot], gzr_sem.at[there], spot(dz=dz))
    mean = gain_z[0]
    for k in range(1, nz):
        mean = mean + gain_z[k]
    mean = mean * (1.0 / replicas)
    group = core * nx + x
    for i in range(2):
        for j in range(4):
            row, lane = i * 4 + j, slice(j * LANES, (j + 1) * LANES)
            part = mean[row : row + 1]
            new_gainm = 0.9 * gainm_ref[i : i + 1, lane] + part
            gainm_out[row : row + 1, :] = new_gainm
            gains[group, row : row + 1, :] = gain_ref[i : i + 1, lane] - 0.02 * (part + 0.9 * new_gainm)
    for slot, dx in enumerate(x_peers):
        send(gains.at[group], gains.at[group], gs_sem.at[slot], gr_sem.at[x], spot(dx=dx))
    bulk(*PLAN[3])
    total = right_send[place]
    for slot in range(len(xy_peers)):
        arrivals[slot].wait_recv()
        total = total + right_recv[slot]
    rmid[z] = total
    for slot, dz in enumerate(z_peers):
        send(rmid.at[z], rmid.at[z], ns_sem.at[slot], nr_sem.at[z], spot(dz=dz))
    other = spot(dc=1)
    for slot in range(1, nx):
        arrive(ortho.at[slot, half], xs_sem.at[slot - 1], xr_sem.at[slot - 1], spot(dx=slot))
    send(ortho.at[1:nx, half], ortho.at[1:nx, half], ps_sem.at[2], pr_sem.at[2], other)
    bulk(*PLAN[4])
    for slot, dz in enumerate(z_peers):
        there = lax.rem(z + dz, nz)
        arrive(rmid.at[there], ns_sem.at[slot], nr_sem.at[there], spot(dz=dz))
    total = rmid[0]
    for k in range(1, nz):
        total = total + rmid[k]
    newb[place] = total * (1.0 / replicas)
    for slot, (dx, dy) in enumerate(xy_peers):
        send(newb.at[place], newb.at[place], as_sem.at[slot], ar_sem.at[place], spot(dy=dy, dx=dx))
    bulk(*PLAN[5])

    otherhalf = pl.ds(other[1] * NY, NY)
    arrive(ortho.at[1:nx, otherhalf], ps_sem.at[2], pr_sem.at[2], other)
    for slot, dx in enumerate(x_peers):
        there = lax.rem(x + dx, nx)
        arrive(gains.at[core * nx + there], gs_sem.at[slot], gr_sem.at[there], spot(dx=dx))
    gsq = jnp.zeros((2 * rank, 2 * rank), F32)
    for s in range(nx):
        for k in range(nc):
            parts = split3(ortho[lax.rem(s + nx - x, nx), k])
            both = jnp.concatenate(parts[0:2], axis=0)
            gsq = gsq + dot(both, both, ((1,), (1,)))
    gsq = gsq[0:rank, 0:rank] + gsq[0:rank, rank:] + gsq[rank:, 0:rank] + gsq[rank:, rank:]
    ortho_out[...] = ortho[...]

    for slot, (dx, dy) in enumerate(xy_peers):
        there = spot(dy=dy, dx=dx)
        index = there[2] * NY + lax.rem(y + dy, NY)
        arrive(newb.at[index], as_sem.at[slot], ar_sem.at[index], there)

    nsq = jnp.zeros((2 * rank, 2 * rank), F32)
    for j in range(across):
        col = jnp.concatenate([newb[i * across + j] for i in range(rank // SUB)], axis=0)
        parts = split3(col)
        both = jnp.concatenate(parts[0:2], axis=0)
        nsq = nsq + dot(both, both, ((1,), (1,)))
    nsq = nsq[0:rank, 0:rank] + nsq[0:rank, rank:] + nsq[rank:, 0:rank] + nsq[rank:, rank:]
    pair_send[...] = jnp.zeros_like(pair_send)
    pair_send[:, 0:rank] = nsq
    pair = send(pair_send, pair_recv, ps_sem.at[0], pr_sem.at[0], other)
    half = pl.ds(core * nx, nx)
    send(gains.at[half], gains.at[half], ps_sem.at[1], pr_sem.at[1], other)
    bulk(*PLAN[6])

    nb_out[...] = newb[...]
    pair.wait_recv()
    square = jnp.sum(gsq * (nsq + pair_recv[:, 0:rank]))
    mean_square = square * (1.0 / (rows * cols * nt * nx))
    scale_out[...] = lax.rsqrt(jnp.full((SUB, LANES), mean_square + 1e-06, F32))
    half = pl.ds(other[1] * nx, nx)
    arrive(gains.at[half], ps_sem.at[1], pr_sem.at[1], other)
    gains_out[...] = gains[...]
    keep.wait()
    bulk(*PLAN[7])
    for copy in sent:
        copy.wait_send()


def apply_kernel(
    sizes, scale_ref, nb_ref, ortho_ref, gains_ref, gainm_ref, moved_ref, g_ref, e_ref, m_ref,
    weight_out, error_out, momentum_out, gain_out, gainm_out, right, left,
):
    nz, nt, nx, rank = sizes
    step = pl.program_id(0)
    x = lax.axis_index("section")
    across = nb_ref.shape[0] // (rank // SUB)
    nc = ortho_ref.shape[1]
    order_right = (0, 1, 2, 0, 1, 0)
    order_left = (0, 0, 0, 1, 1, 2)

    @pl.when(step == 0)
    def _():
        for j in range(across):
            col = jnp.concatenate([nb_ref[i * across + j] for i in range(rank // SUB)], axis=0)
            parts = split3(col)
            for p in range(6):
                right[p * rank : (p + 1) * rank, j * LANES : (j + 1) * LANES] = parts[order_right[p]]
        for t in range(nt * nx):
            for i in range(2):
                for j in range(4):
                    at = (t * 4 + j) * LANES
                    gain_out[i : i + 1, at : at + LANES] = gains_ref[t, i * 4 + j : i * 4 + j + 1, :]
        for i in range(2):
            for j in range(4):
                gainm_out[i : i + 1, j * LANES : (j + 1) * LANES] = gainm_ref[i * 4 + j : i * 4 + j + 1, :]

    scale = scale_ref[0:1, 0:1]
    size = m_ref.shape[0]
    per = size // LANES

    def product(s):
        for q in range(per):
            parts = split3(ortho_ref[s, step * per + q])
            for p in range(6):
                left[p * rank : (p + 1) * rank, q * LANES : (q + 1) * LANES] = parts[order_left[p]]
        return dot(left[...], right[...], ((0,), (0,)))

    for r in range(nx):
        approx = product(r)
        weight_out[lax.rem(x + r, nx)] = (moved_ref[r] - (0.095 * scale) * approx).astype(BF16)
        if r == 0:
            error_out[0] = (g_ref[0].astype(F32) + e_ref[0].astype(F32) - approx).astype(BF16)
            momentum_out[...] = 0.9 * m_ref[...] + scale * approx


def on_device(weight, grads, error, momentum, basis, gram_root, gain, gain_momentum, gain_grads):
    replicas = lax.axis_size("replica")
    nt = lax.axis_size("tensor")
    nx = lax.axis_size("section")
    rows, cols = weight.shape
    rank = gram_root.shape[0]
    nz = replicas // NY
    sizes = (nz, nt, nx, rank)
    nc = nt * NY
    nxy = nx * NY
    chunk = rows // nc
    vmem = pl.BlockSpec(memory_space=pltpu.VMEM)
    hbm = pl.BlockSpec(memory_space=pl.ANY)
    dma = pltpu.SemaphoreType.DMA
    scale, newb, ortho, gains, gainm, moved = pl.pallas_call(
        functools.partial(exchange_kernel, sizes),
        out_shape=(
            jax.ShapeDtypeStruct((SUB, LANES), F32),
            jax.ShapeDtypeStruct((nxy, SUB, LANES), F32),
            jax.ShapeDtypeStruct((nx, nc, rank, chunk), F32),
            jax.ShapeDtypeStruct((nt * nx, SUB, LANES), F32),
            jax.ShapeDtypeStruct((SUB, LANES), F32),
            jax.ShapeDtypeStruct((nx, rows, cols), F32),
        ),
        in_specs=[pl.BlockSpec(memory_space=pltpu.HBM)] * 9,
        out_specs=(vmem, vmem, vmem, vmem, vmem, hbm),
        scratch_shapes=[
            pltpu.VMEM((rows, cols), BF16),
            pltpu.VMEM((rows, cols), BF16),
            pltpu.VMEM((rows, cols), BF16),
            pltpu.VMEM((rows, cols), F32),
            pltpu.VMEM((rank, cols), F32),
            pltpu.VMEM((rank, rank), F32),
            pltpu.VMEM((1, 2, cols), F32),
            pltpu.VMEM((2, cols), F32),
            pltpu.VMEM((2, cols), F32),
            pltpu.VMEM((rows, cols), F32),
            pltpu.VMEM((3 * rank, cols), BF16),
            pltpu.VMEM((3 * rank, rows), BF16),
            pltpu.VMEM((nc, rank, chunk), F32),
            pltpu.VMEM((nc - 1, rank, chunk), F32),
            pltpu.VMEM((nz, rank, chunk), F32),
            pltpu.VMEM((nx, nc, rank, chunk), F32),
            pltpu.VMEM((nxy, SUB, LANES), F32),
            pltpu.VMEM((nxy - 1, SUB, LANES), F32),
            pltpu.VMEM((nz, SUB, LANES), F32),
            pltpu.VMEM((nxy, SUB, LANES), F32),
            pltpu.VMEM((nt * nx, SUB, LANES), F32),
            pltpu.VMEM((NY, SUB, LANES), F32),
            pltpu.VMEM((nz, SUB, LANES), F32),
            pltpu.VMEM((rank, LANES), F32),
            pltpu.VMEM((rank, LANES), F32),
            dma((10,)),
            dma((nc,)), dma((nc,)),
            dma((nz,)), dma((nz,)),
            dma((nc,)), dma((nc,)),
            dma((nx,)), dma((nx,)),
            dma((nxy,)), dma((nxy,)),
            dma((nz,)), dma((nz,)),
            dma((nxy,)), dma((nxy,)),
            dma((nx,)), dma((nx,)),
            dma((nx,)), dma((nx,)),
            dma((3,)), dma((3,)),
            dma((NY,)), dma((NY,)),
            dma((nz,)), dma((nz,)),
            dma((COUNT, 5)), dma((COUNT, 5)),
        ],
        compiler_params=pltpu.CompilerParams(
            collective_id=0, has_side_effects=True, vmem_limit_bytes=24 * 1024 * 1024
        ),
    )(
        *[
            pltpu.with_memory_space_constraint(operand, pltpu.HBM)
            for operand in (grads, error, weight, momentum, basis.T, gram_root, gain_grads, gain, gain_momentum)
        ]
    )
    size = 256
    new_weight, new_error, new_momentum, new_gain, new_gainm = pl.pallas_call(
        functools.partial(apply_kernel, sizes),
        grid=(rows // size,),
        out_shape=(
            jax.ShapeDtypeStruct((nx, rows, cols), BF16),
            jax.ShapeDtypeStruct((1, rows, cols), BF16),
            jax.ShapeDtypeStruct((rows, cols), F32),
            jax.ShapeDtypeStruct((2, nt * nx * 4 * LANES), F32),
            jax.ShapeDtypeStruct((2, 4 * LANES), F32),
        ),
        in_specs=[
            vmem, vmem, vmem, vmem, vmem,
            pl.BlockSpec((nx, size, cols), lambda i: (0, i, 0)),
            pl.BlockSpec((1, size, cols), lambda i: (0, i, 0)),
            pl.BlockSpec((1, size, cols), lambda i: (0, i, 0)),
            pl.BlockSpec((size, cols), lambda i: (i, 0)),
        ],
        out_specs=(
            pl.BlockSpec((nx, size, cols), lambda i: (0, i, 0)),
            pl.BlockSpec((1, size, cols), lambda i: (0, i, 0)),
            pl.BlockSpec((size, cols), lambda i: (i, 0)),
            vmem,
            vmem,
        ),
        scratch_shapes=[pltpu.VMEM((6 * rank, cols), BF16), pltpu.VMEM((6 * rank, size), BF16)],
        compiler_params=pltpu.CompilerParams(vmem_limit_bytes=24 * 1024 * 1024),
    )(scale, newb, ortho, gains, gainm, moved, grads, error, momentum)
    return (new_weight.reshape(nx * rows, cols), new_error, new_momentum, new_gain, new_gainm)


def solution(mesh):
    placed = (
        P("section", "tensor"),
        P("replica", "section", "tensor"),
        P("replica", "section", "tensor"),
        P("section", "tensor"),
        P("tensor", None),
        P(),
        P(None, ("tensor", "section")),
        P(None, ("tensor", "section")),
        P("replica", None, ("tensor", "section")),
    )
    return jax.shard_map(
        on_device,
        mesh=mesh,
        in_specs=placed,
        out_specs=(
            P(None, "tensor"),
            P("replica", "section", "tensor"),
            P("section", "tensor"),
            P(),
            P(None, ("tensor", "section")),
        ),
        check_vma=False,
    )
```

```python
import functools

import jax
import jax.numpy as jnp
from jax import lax
from jax.experimental import pallas as pl
from jax.experimental.pallas import tpu as pltpu
from jax.sharding import PartitionSpec as P

MESH = pl.DeviceIdType.MESH
F32 = jnp.float32
BF16 = jnp.bfloat16
HIGHEST = lax.Precision.HIGHEST
NY = 4
LANES = 128
SUB = 8
PIECE = 16
PARTS = 4
ORDER = (
    "y++", "y--", "z+-", "z-+", "y+-", "y-+", "z++", "z--", "y++", "y--", "z+-", "z-+", "y+-", "y-+",
)
TAIL = 2
COUNT = len(ORDER)


def ops(*words):
    found = []
    for word in words:
        name = word.rstrip("0123456789")
        number = word[len(name) :]
        found.append((name, int(number) if number else 0))
    return found


PLAN = (
    ops("x0", "x1", "x2", "x3", "r0", "x4", "r1", "x5"),
    ops("r2", "x6", "r3", "x7", "a0", "a1", "r4", "x8", "r5", "x9", "a2", "a3", "r6", "x10"),
    ops("r7", "x11", "b0", "a4", "b1", "a5", "r8", "x12", "r9", "x13", "a6", "a7", "r10", "r11"),
    ops("ox", "b2", "b3", "a8", "a9", "r12", "r13", "X0", "a10", "a11"),
    ops("oa", "b4", "b5", "a12", "a13", "b8", "b9"),
    ops("ob", "b6", "b7", "b10", "b11", "X1", "b12", "b13"),
    ops(),
    ops("op")
    + ops("ow") + [("w", j) for j in range(COUNT)] + [("XW", j) for j in range(TAIL)],
)


def split3(value):
    first = value.astype(BF16)
    rest = value - first.astype(F32)
    second = rest.astype(BF16)
    third = (rest - second.astype(F32)).astype(BF16)
    return first, second, third


def dot(left, right, dims):
    return lax.dot_general(left, right, (dims, ((), ())), preferred_element_type=F32)


def exchange_kernel(
    sizes,
    grads_ref, error_ref, weight_ref, momentum_ref, basis_in, gram_in, gaing_in, gain_in, gainm_in,
    scale_out, nb_out, ortho_out, gains_out, gainm_out, g_buf, e_buf, m_buf, c_buf, moved_ref,
    w_buf, basis_ref, gram_ref, gaing_ref, gain_ref, gainm_ref,
    pieces, opieces, left_send, left_recv, mid_recv, ortho, right_send, right_recv,
    rmid, newb, gains, gain_y, gain_z, pair_recv,
    load_sem, ls_sem, lr_sem, ms_sem, mr_sem, os_sem, or_sem, xs_sem, xr_sem,
    rs_sem, rr_sem, ns_sem, nr_sem, as_sem, ar_sem, bs_sem, br_sem, gs_sem, gr_sem, ps_sem, pr_sem,
    gys_sem, gyr_sem, gzs_sem, gzr_sem, qs_sem, qr_sem,
):
    nz, nt, nx, rank = sizes
    replicas = nz * NY
    rep = lax.axis_index("replica")
    core = lax.axis_index("tensor")
    x = lax.axis_index("section")
    z = rep // NY
    y = rep % NY
    rows, cols = c_buf.shape
    nc = nt * NY
    steps = rows // nc

    def load(source, target):
        copy = pltpu.make_async_copy(source, target, load_sem.at[len(loads)])
        copy.start()
        loads.append(copy)

    loads = []
    load(basis_in, basis_ref)
    fold = rows // PARTS
    for k in range(PARTS):
        part = pl.ds(k * fold, fold)
        load(grads_ref.at[0, part], g_buf.at[part])
        load(error_ref.at[0, part], e_buf.at[part])

    def spot(dz=0, dy=0, dc=0, dx=0):
        return (lax.rem(z + dz, nz) * NY + lax.rem(y + dy, NY), lax.rem(core + dc, nt), lax.rem(x + dx, nx))

    cy_peers = [(dc, dy) for dc in range(nt) for dy in range(NY) if (dc, dy) != (0, 0)]
    xy_peers = [(dx, dy) for dx in range(nx) for dy in range(NY) if (dx, dy) != (0, 0)]
    cy_peers.sort(key=lambda p: (-min(p[1], NY - p[1]), -p[0]))
    xy_peers.sort(key=lambda p: -min(p[1], NY - p[1]) - min(p[0], nx - p[0]))
    z_peers = sorted(range(1, nz), key=lambda d: -min(d, nz - d))
    all_peers = [(0, 1, 0)] + [(dx, dc, dy) for dx, dy in xy_peers for dc in range(nt)]
    x_peers = (2, 1, 3)
    y_peers = (2, 1, 3)
    cx_peers = [(dx, dc) for dx in range(nx) for dc in range(nt) if (dx, dc) != (0, 0)]
    greet = {(0, dy, dc, 0) for dc, dy in cy_peers} | {(0, dy, 0, dx) for dx, dy in xy_peers}
    greet |= {(dz, 0, 0, 0) for dz in z_peers} | {(0, dy, 1, dx) for dx in range(nx) for dy in range(NY)}
    greet = sorted(greet)

    barrier = pltpu.get_barrier_semaphore()
    for dz, dy, dc, dx in greet:
        pl.semaphore_signal(barrier, inc=1, device_id=spot(dz, dy, dc, dx), device_id_type=MESH)

    sent = []

    def send(source, target, ssem, rsem, there):
        copy = pltpu.make_async_remote_copy(
            src_ref=source, dst_ref=target, send_sem=ssem, recv_sem=rsem, device_id=there, device_id_type=MESH
        )
        copy.start()
        sent.append(copy)
        return copy

    def arrive(target, ssem, rsem, there):
        pltpu.make_async_remote_copy(
            src_ref=target, dst_ref=target, send_sem=ssem, recv_sem=rsem, device_id=there, device_id_type=MESH
        ).wait_recv()

    ybit = y % 2
    zbit = z % 2

    def plan(j):
        kind = ORDER[j]
        dy = 1 - 2 * ybit if kind[1] == "+" else 2 * ybit - 1
        dz = 1 - 2 * zbit if kind[2] == "+" else 2 * zbit - 1
        to_y = spot(dy=dy + NY)
        to_z = spot(dz=dz + nz)
        if kind[0] == "y":
            return ybit, zbit, to_y, to_z
        return zbit, ybit, to_z, to_y

    def block(j, start, size):
        return pl.ds(pl.multiple_of(j * 4 * PIECE + start, PIECE), size)

    def bulk(*ops):
        for kind, j in ops:
            if kind[0] == "X":
                size = (rows - len(ORDER) * 4 * PIECE) // TAIL
                tail = pl.ds(len(ORDER) * 4 * PIECE + j * size, size)
                if kind == "X":
                    for slot, dx in enumerate(x_peers):
                        send(
                            c_buf.at[tail], moved_ref.at[nx - dx - 1, tail],
                            bs_sem.at[j, slot], br_sem.at[j, nx - dx - 1], spot(dx=dx),
                        )
                if kind == "XW":
                    for slot in range(1, nx):
                        arrive(moved_ref.at[slot - 1, tail], bs_sem.at[j, slot - 1], br_sem.at[j, slot - 1], spot(dx=slot))
                continue
            if kind[0] == "o":
                piece = core * 4 + 2 * zbit + ybit
                to_y, to_z = plan(0)[2:]
                if kind == "ox":
                    for slot, dx in enumerate(x_peers):
                        send(
                            ortho.at[0, piece], ortho.at[nx - dx, piece],
                            xs_sem.at[slot], xr_sem.at[nx - dx - 1], spot(dx=dx),
                        )
                if kind == "oa":
                    for slot in range(1, nx):
                        arrive(ortho.at[slot, piece], xs_sem.at[slot - 1], xr_sem.at[slot - 1], spot(dx=slot))
                    send(ortho.at[1:nx, piece], ortho.at[1:nx, piece], xs_sem.at[3], xr_sem.at[3], to_y)
                if kind == "ob":
                    near = core * 4 + 2 * zbit + 1 - ybit
                    arrive(ortho.at[1:nx, near], xs_sem.at[3], xr_sem.at[3], to_y)
                    pair = pl.ds(core * 4 + 2 * zbit, 2)
                    send(ortho.at[1:nx, pair], ortho.at[1:nx, pair], xs_sem.at[4], xr_sem.at[4], to_z)
                if kind == "op":
                    pair = pl.ds(core * 4 + 2 * (1 - zbit), 2)
                    arrive(ortho.at[1:nx, pair], xs_sem.at[4], xr_sem.at[4], to_z)
                    send(ortho.at[1:nx, half], ortho.at[1:nx, half], ps_sem.at[0], pr_sem.at[0], other)
                if kind == "ow":
                    arrive(ortho.at[1:nx, otherhalf], ps_sem.at[0], pr_sem.at[0], other)
                continue
            low, high, first, second = plan(j)
            mine = block(j, PIECE * (2 * high + low), PIECE)
            theirs = block(j, PIECE * (2 * high + 1 - low), PIECE)
            both = block(j, 2 * PIECE * high, 2 * PIECE)
            rest = block(j, 2 * PIECE * (1 - high), 2 * PIECE)
            if kind == "x":
                for slot, dx in ((0, 1), (1, nx - 1)):
                    send(c_buf.at[mine], moved_ref.at[nx - dx - 1, mine], qs_sem.at[j, slot], qr_sem.at[j, nx - dx - 1], spot(dx=dx))
            near, far = ((0, 2), (2, 0))[j % 2]
            if kind == "r":
                arrive(moved_ref.at[near, mine], qs_sem.at[j, 0], qr_sem.at[j, near], spot(dx=near + 1))
                send(moved_ref.at[near, mine], moved_ref.at[1, mine], qs_sem.at[j, 2], qr_sem.at[j, 1], spot(dx=far + 1))
            if kind == "a":
                for slot in (far, 1):
                    arrive(moved_ref.at[slot, mine], qs_sem.at[j, slot], qr_sem.at[j, slot], spot(dx=slot + 1))
                send(moved_ref.at[:, mine], moved_ref.at[:, mine], qs_sem.at[j, 3], qr_sem.at[j, 3], first)
            if kind == "b":
                arrive(moved_ref.at[:, theirs], qs_sem.at[j, 3], qr_sem.at[j, 3], first)
                send(moved_ref.at[:, both], moved_ref.at[:, both], qs_sem.at[j, 4], qr_sem.at[j, 4], second)
            if kind == "w":
                arrive(moved_ref.at[:, rest], qs_sem.at[j, 4], qr_sem.at[j, 4], second)

    mine = core * NY + y
    other = spot(dc=1)
    half = pl.ds(core * NY, NY)
    otherhalf = pl.ds(other[1] * NY, NY)

    loads[0].wait()
    b1, b2, b3 = split3(basis_ref[...])
    pieces[0:rank, :] = b1
    pieces[rank : 2 * rank, :] = b2
    pieces[2 * rank : 3 * rank, :] = b3
    for k in range(PARTS):
        loads[1 + 2 * k].wait()
        loads[2 + 2 * k].wait()
        if k == 1:
            for source, target in (
                (weight_ref, w_buf), (momentum_ref, m_buf), (gaing_in, gaing_ref),
                (gram_in, gram_ref), (gain_in, gain_ref), (gainm_in, gainm_ref),
            ):
                load(source, target)
        part = pl.ds(k * fold, fold)
        low = dot(pieces[...], g_buf[part, :], ((1,), (1,))) + dot(pieces[...], e_buf[part, :], ((1,), (1,)))
        low = low[0:rank] + low[rank : 2 * rank] + low[2 * rank : 3 * rank]
        for i in range(fold // steps):
            left_send[k * fold // steps + i] = low[:, i * steps : (i + 1) * steps]

    pl.semaphore_wait(barrier, len(greet))

    arrivals = []
    for slot, (dc, dy) in enumerate(cy_peers):
        there = spot(dy=dy, dc=dc)
        arrivals.append(
            send(left_send.at[there[1] * NY + lax.rem(y + dy, NY)], left_recv.at[slot], ls_sem.at[slot], lr_sem.at[slot], there)
        )
    for copy in loads[1 + 2 * PARTS :]:
        copy.wait()
    for i in range(2):
        for j in range(4):
            row = i * 4 + j
            gain_y[y, row : row + 1, :] = gaing_ref[0, i : i + 1, j * LANES : (j + 1) * LANES]
    c_buf[...] = w_buf[...].astype(F32) - 0.0405 * m_buf[...]
    for slot, dy in enumerate(y_peers):
        send(gain_y.at[y], gain_y.at[y], gys_sem.at[slot], gyr_sem.at[y], spot(dy=dy))
    bulk(*PLAN[0])

    total = left_send[mine]
    for slot in range(len(cy_peers)):
        arrivals[slot].wait_recv()
        total = total + left_recv[slot]
    mid_recv[z] = total
    for slot, dz in enumerate(z_peers):
        send(mid_recv.at[z], mid_recv.at[z], ms_sem.at[slot], mr_sem.at[z], spot(dz=dz))
    for slot, dy in enumerate(y_peers):
        there = lax.rem(y + dy, NY)
        arrive(gain_y.at[there], gys_sem.at[slot], gyr_sem.at[there], spot(dy=dy))
    gain_z[z] = ((gain_y[0] + gain_y[1]) + gain_y[2]) + gain_y[3]
    bulk(*PLAN[1])
    for slot, dz in enumerate(z_peers):
        there = lax.rem(z + dz, nz)
        arrive(mid_recv.at[there], ms_sem.at[slot], mr_sem.at[there], spot(dz=dz))
    total = mid_recv[0]
    for k in range(1, nz):
        total = total + mid_recv[k]
    ortho[0, mine] = lax.dot_general(
        gram_ref[...], total * (1.0 / replicas), (((0,), (0,)), ((), ())), precision=HIGHEST, preferred_element_type=F32
    )
    for slot, (dc, dy) in enumerate(cy_peers):
        send(ortho.at[0, mine], ortho.at[0, mine], os_sem.at[slot], or_sem.at[mine], spot(dy=dy, dc=dc))
    for slot, dz in enumerate(z_peers):
        send(gain_z.at[z], gain_z.at[z], gzs_sem.at[slot], gzr_sem.at[z], spot(dz=dz))
    bulk(*PLAN[2])
    for slot, (dc, dy) in enumerate(cy_peers):
        there = spot(dy=dy, dc=dc)
        index = there[1] * NY + lax.rem(y + dy, NY)
        arrive(ortho.at[0, index], os_sem.at[slot], or_sem.at[index], there)

    for k in range(nc):
        parts = split3(ortho[0, k])
        for p in range(3):
            opieces[p * rank : (p + 1) * rank, k * steps : (k + 1) * steps] = parts[p]
    right = dot(opieces[...], g_buf[...], ((1,), (0,))) + dot(opieces[...], e_buf[...], ((1,), (0,)))
    right = right[0:rank] + right[rank : 2 * rank] + right[2 * rank : 3 * rank]
    across = cols // LANES
    for i in range(rank // SUB):
        for j in range(across):
            right_send[i * across + j] = right[i * SUB : (i + 1) * SUB, j * LANES : (j + 1) * LANES]

    place = x * NY + y
    arrivals = []
    for slot, (dx, dy) in enumerate(xy_peers):
        there = spot(dy=dy, dx=dx)
        arrivals.append(
            send(right_send.at[there[2] * NY + lax.rem(y + dy, NY)], right_recv.at[slot], rs_sem.at[slot], rr_sem.at[slot], there)
        )
    gram_own = jnp.zeros((2 * rank, 2 * rank), F32)
    for k in range(nc):
        both = opieces[0 : 2 * rank, k * steps : (k + 1) * steps]
        gram_own = gram_own + dot(both, both, ((1,), (1,)))
    pair_recv[x] = jnp.zeros((rank, LANES), F32)
    pair_recv[x, :, 0:rank] = (gram_own[0:rank, 0:rank] + gram_own[rank:, rank:]) + (
        gram_own[0:rank, rank:] + gram_own[rank:, 0:rank]
    )
    for slot, dx in enumerate(x_peers):
        send(pair_recv.at[x], pair_recv.at[x], ps_sem.at[1 + slot], pr_sem.at[1 + x], spot(dx=dx))
    bulk(*PLAN[3])
    total = right_send[place]
    for slot in range(len(xy_peers)):
        arrivals[slot].wait_recv()
        total = total + right_recv[slot]
    rmid[z] = total
    for slot, dz in enumerate(z_peers):
        send(rmid.at[z], rmid.at[z], ns_sem.at[slot], nr_sem.at[z], spot(dz=dz))
    for slot, dz in enumerate(z_peers):
        there = lax.rem(z + dz, nz)
        arrive(gain_z.at[there], gzs_sem.at[slot], gzr_sem.at[there], spot(dz=dz))
    mean = gain_z[0]
    for k in range(1, nz):
        mean = mean + gain_z[k]
    mean = mean * (1.0 / replicas)
    group = core * nx + x
    for i in range(2):
        for j in range(4):
            row, lane = i * 4 + j, slice(j * LANES, (j + 1) * LANES)
            part = mean[row : row + 1]
            new_gainm = 0.9 * gainm_ref[i : i + 1, lane] + part
            gainm_out[row : row + 1, :] = new_gainm
            gains[group, row : row + 1, :] = gain_ref[i : i + 1, lane] - 0.02 * (part + 0.9 * new_gainm)
    for slot, (dx, dc) in enumerate(cx_peers):
        send(gains.at[group], gains.at[group], gs_sem.at[slot], gr_sem.at[group], spot(dx=dx, dc=dc))
    bulk(*PLAN[4])
    for slot, dz in enumerate(z_peers):
        there = lax.rem(z + dz, nz)
        arrive(rmid.at[there], ns_sem.at[slot], nr_sem.at[there], spot(dz=dz))
    total = rmid[0]
    for k in range(1, nz):
        total = total + rmid[k]
    newb[core, place] = total * (1.0 / replicas)
    for slot, (dx, dc, dy) in enumerate(all_peers):
        send(
            newb.at[core, place], newb.at[core, place], as_sem.at[slot], ar_sem.at[core, place],
            spot(dy=dy, dx=dx, dc=dc),
        )
    bulk(*PLAN[5])

    for slot, dx in enumerate(x_peers):
        there = lax.rem(x + dx, nx)
        arrive(pair_recv.at[there], ps_sem.at[1 + slot], pr_sem.at[1 + there], spot(dx=dx))
    gsq = pair_recv[0]
    for s in range(1, nx):
        gsq = gsq + pair_recv[s]
    for slot, (dx, dc) in enumerate(cx_peers):
        there = spot(dx=dx, dc=dc)
        index = there[1] * nx + there[2]
        arrive(gains.at[index], gs_sem.at[slot], gr_sem.at[index], there)
    gains_out[...] = gains[...]
    bulk(*PLAN[6])
    for slot, (dx, dc, dy) in enumerate(all_peers):
        there = spot(dy=dy, dx=dx, dc=dc)
        index = there[2] * NY + lax.rem(y + dy, NY)
        arrive(newb.at[there[1], index], as_sem.at[slot], ar_sem.at[there[1], index], there)

    nsq = jnp.zeros((2 * rank, 2 * rank), F32)
    for c in range(nt):
        for j in range(across):
            col = jnp.concatenate([newb[c, i * across + j] for i in range(rank // SUB)], axis=0)
            parts = split3(col)
            both = jnp.concatenate(parts[0:2], axis=0)
            nsq = nsq + dot(both, both, ((1,), (1,)))
    nsq = (nsq[0:rank, 0:rank] + nsq[rank:, rank:]) + (nsq[0:rank, rank:] + nsq[rank:, 0:rank])
    nb_out[...] = newb[core]
    square = jnp.sum(gsq[:, 0:rank] * nsq)
    mean_square = square * (1.0 / (rows * cols * nt * nx))
    scale_out[...] = lax.rsqrt(jnp.full((SUB, LANES), mean_square + 1e-06, F32))
    bulk(*PLAN[7])
    ortho_out[...] = ortho[...]
    for copy in sent:
        copy.wait_send()


def apply_kernel(
    sizes, scale_ref, nb_ref, ortho_ref, gains_ref, gainm_ref, c_ref, moved_ref, g_ref, e_ref, m_ref,
    weight_out, error_out, momentum_out, gain_out, gainm_out, right, left,
):
    nz, nt, nx, rank = sizes
    step = pl.program_id(0)
    x = lax.axis_index("section")
    across = nb_ref.shape[0] // (rank // SUB)
    nc = ortho_ref.shape[1]
    order_right = (0, 1, 0)
    order_left = (0, 0, 1)

    @pl.when(step == 0)
    def _():
        for j in range(across):
            col = jnp.concatenate([nb_ref[i * across + j] for i in range(rank // SUB)], axis=0)
            parts = split3(col)
            for p in range(3):
                right[p * rank : (p + 1) * rank, j * LANES : (j + 1) * LANES] = parts[order_right[p]]
        for t in range(nt * nx):
            for i in range(2):
                for j in range(4):
                    at = (t * 4 + j) * LANES
                    gain_out[i : i + 1, at : at + LANES] = gains_ref[t, i * 4 + j : i * 4 + j + 1, :]
        for i in range(2):
            for j in range(4):
                gainm_out[i : i + 1, j * LANES : (j + 1) * LANES] = gainm_ref[i * 4 + j : i * 4 + j + 1, :]

    scale = scale_ref[0:1, 0:1]
    size = momentum_out.shape[0]
    here = pl.ds(pl.multiple_of(step * size, size), size)
    per = size // LANES

    def product(s):
        for q in range(per):
            parts = split3(ortho_ref[s, step * per + q])
            for p in range(3):
                left[p * rank : (p + 1) * rank, q * LANES : (q + 1) * LANES] = parts[order_left[p]]
        return dot(left[...], right[...], ((0,), (0,)))

    for r in range(nx):
        approx = product(r)
        base = moved_ref[r - 1, here, :] if r else c_ref[here, :]
        weight_out[lax.rem(x + r, nx)] = (base - (0.095 * scale) * approx).astype(BF16)
        if r == 0:
            error_out[0] = (g_ref[here, :].astype(F32) + e_ref[here, :].astype(F32) - approx).astype(BF16)
            momentum_out[...] = 0.9 * m_ref[here, :] + scale * approx


def on_device(weight, grads, error, momentum, basis, gram_root, gain, gain_momentum, gain_grads):
    replicas = lax.axis_size("replica")
    nt = lax.axis_size("tensor")
    nx = lax.axis_size("section")
    rows, cols = weight.shape
    rank = gram_root.shape[0]
    nz = replicas // NY
    sizes = (nz, nt, nx, rank)
    nc = nt * NY
    nxy = nx * NY
    chunk = rows // nc
    vmem = pl.BlockSpec(memory_space=pltpu.VMEM)
    hbm = pl.BlockSpec(memory_space=pl.ANY)
    dma = pltpu.SemaphoreType.DMA
    scale, newb, ortho, gains, gainm, g_here, e_here, m_here, c_here, moved = pl.pallas_call(
        functools.partial(exchange_kernel, sizes),
        out_shape=(
            jax.ShapeDtypeStruct((SUB, LANES), F32),
            jax.ShapeDtypeStruct((nxy, SUB, LANES), F32),
            jax.ShapeDtypeStruct((nx, nc, rank, chunk), F32),
            jax.ShapeDtypeStruct((nt * nx, SUB, LANES), F32),
            jax.ShapeDtypeStruct((SUB, LANES), F32),
            jax.ShapeDtypeStruct((rows, cols), BF16),
            jax.ShapeDtypeStruct((rows, cols), BF16),
            jax.ShapeDtypeStruct((rows, cols), F32),
            jax.ShapeDtypeStruct((rows, cols), F32),
            jax.ShapeDtypeStruct((nx - 1, rows, cols), F32),
        ),
        in_specs=[pl.BlockSpec(memory_space=pltpu.HBM)] * 9,
        out_specs=(vmem,) * 9 + (hbm,),
        scratch_shapes=[
            pltpu.VMEM((rows, cols), BF16),
            pltpu.VMEM((rank, cols), F32),
            pltpu.VMEM((rank, rank), F32),
            pltpu.VMEM((1, 2, cols), F32),
            pltpu.VMEM((2, cols), F32),
            pltpu.VMEM((2, cols), F32),
            pltpu.VMEM((3 * rank, cols), BF16),
            pltpu.VMEM((3 * rank, rows), BF16),
            pltpu.VMEM((nc, rank, chunk), F32),
            pltpu.VMEM((nc - 1, rank, chunk), F32),
            pltpu.VMEM((nz, rank, chunk), F32),
            pltpu.VMEM((nx, nc, rank, chunk), F32),
            pltpu.VMEM((nxy, SUB, LANES), F32),
            pltpu.VMEM((nxy - 1, SUB, LANES), F32),
            pltpu.VMEM((nz, SUB, LANES), F32),
            pltpu.VMEM((nt, nxy, SUB, LANES), F32),
            pltpu.VMEM((nt * nx, SUB, LANES), F32),
            pltpu.VMEM((NY, SUB, LANES), F32),
            pltpu.VMEM((nz, SUB, LANES), F32),
            pltpu.VMEM((nx, rank, LANES), F32),
            dma((8 + 2 * PARTS,)),
            dma((nc,)), dma((nc,)),
            dma((nz,)), dma((nz,)),
            dma((nc,)), dma((nc,)),
            dma((5,)), dma((5,)),
            dma((nxy,)), dma((nxy,)),
            dma((nz,)), dma((nz,)),
            dma((nt * nxy,)), dma((nt, nxy)),
            dma((TAIL, nx)), dma((TAIL, nx)),
            dma((nt * nx,)), dma((nt * nx,)),
            dma((1 + nx,)), dma((1 + nx,)),
            dma((NY,)), dma((NY,)),
            dma((nz,)), dma((nz,)),
            dma((COUNT, 5)), dma((COUNT, 5)),
        ],
        compiler_params=pltpu.CompilerParams(
            collective_id=0, has_side_effects=True, vmem_limit_bytes=24 * 1024 * 1024
        ),
    )(
        *[
            pltpu.with_memory_space_constraint(operand, pltpu.HBM)
            for operand in (grads, error, weight, momentum, basis.T, gram_root, gain_grads, gain, gain_momentum)
        ]
    )
    size = 256
    new_weight, new_error, new_momentum, new_gain, new_gainm = pl.pallas_call(
        functools.partial(apply_kernel, sizes),
        grid=(rows // size,),
        out_shape=(
            jax.ShapeDtypeStruct((nx, rows, cols), BF16),
            jax.ShapeDtypeStruct((1, rows, cols), BF16),
            jax.ShapeDtypeStruct((rows, cols), F32),
            jax.ShapeDtypeStruct((2, nt * nx * 4 * LANES), F32),
            jax.ShapeDtypeStruct((2, 4 * LANES), F32),
        ),
        in_specs=[
            vmem, vmem, vmem, vmem, vmem, vmem, vmem, vmem, vmem, vmem,
        ],
        out_specs=(
            pl.BlockSpec((nx, size, cols), lambda i: (0, i, 0)),
            pl.BlockSpec((1, size, cols), lambda i: (0, i, 0)),
            pl.BlockSpec((size, cols), lambda i: (i, 0)),
            vmem,
            vmem,
        ),
        scratch_shapes=[pltpu.VMEM((3 * rank, cols), BF16), pltpu.VMEM((3 * rank, size), BF16)],
        compiler_params=pltpu.CompilerParams(vmem_limit_bytes=24 * 1024 * 1024),
    )(scale, newb, ortho, gains, gainm, c_here, moved, g_here, e_here, m_here)
    return (new_weight.reshape(nx * rows, cols), new_error, new_momentum, new_gain, new_gainm)


def solution(mesh):
    placed = (
        P("section", "tensor"),
        P("replica", "section", "tensor"),
        P("replica", "section", "tensor"),
        P("section", "tensor"),
        P("tensor", None),
        P(),
        P(None, ("tensor", "section")),
        P(None, ("tensor", "section")),
        P("replica", None, ("tensor", "section")),
    )
    return jax.shard_map(
        on_device,
        mesh=mesh,
        in_specs=placed,
        out_specs=(
            P(None, "tensor"),
            P("replica", "section", "tensor"),
            P("section", "tensor"),
            P(),
            P(None, ("tensor", "section")),
        ),
        check_vma=False,
    )
```

```python
import functools

import jax
import jax.numpy as jnp
from jax import lax
from jax.experimental import pallas as pl
from jax.experimental.pallas import tpu as pltpu
from jax.sharding import PartitionSpec as P

MESH = pl.DeviceIdType.MESH
F32 = jnp.float32
BF16 = jnp.bfloat16
HIGHEST = lax.Precision.HIGHEST
NY = 4
LANES = 128
SUB = 8
PIECE = 16
PARTS = 2
ORDER = (
    "y++", "y--", "z+-", "z-+", "y+-", "y-+", "z++", "z--", "y++", "y--", "z+-", "z-+", "y+-", "y-+",
)
TAIL = 2
COUNT = len(ORDER)


def ops(*words):
    found = []
    for word in words:
        name = word.rstrip("0123456789")
        number = word[len(name) :]
        found.append((name, int(number) if number else 0))
    return found


PLAN = (
    ops("x0", "x1", "x2", "x3", "r0", "x4", "r1", "x5"),
    ops("r2", "x6", "r3", "x7", "a0", "a1", "r4", "x8", "r5", "x9", "a2", "a3", "r6", "x10"),
    ops("r7", "x11", "b0", "a4", "b1", "a5", "r8", "x12", "r9", "x13", "a6", "a7", "r10", "r11"),
    ops("b2", "b3", "a8", "a9", "r12", "r13", "ox", "a10", "a11"),
    ops("X0", "b4", "b5", "a12", "a13"),
    ops("op", "b6", "b7", "b8", "b9", "b10", "b11", "X1", "b12", "b13"),
    ops("ow"),
    [("w", j) for j in range(COUNT)] + [("XW", j) for j in range(TAIL)],
)


def split3(value):
    first = value.astype(BF16)
    rest = value - first.astype(F32)
    second = rest.astype(BF16)
    third = (rest - second.astype(F32)).astype(BF16)
    return first, second, third


def dot(left, right, dims):
    return lax.dot_general(left, right, (dims, ((), ())), preferred_element_type=F32)


def exchange_kernel(
    sizes,
    grads_ref, error_ref, weight_ref, momentum_ref, basis_in, gram_in, gaing_in, gain_in, gainm_in,
    scale_out, nb_out, ortho_out, gains_out, gainm_out, g_buf, e_buf, m_buf, c_buf, moved_ref,
    w_buf, basis_ref, gram_ref, gaing_ref, gain_ref, gainm_ref,
    pieces, opieces, left_send, left_recv, mid_recv, ortho, right_send, right_recv,
    rmid, newb, gains, gain_y, gain_z, pair_recv,
    load_sem, ls_sem, lr_sem, ms_sem, mr_sem, os_sem, or_sem, xs_sem, xr_sem,
    rs_sem, rr_sem, ns_sem, nr_sem, as_sem, ar_sem, bs_sem, br_sem, gs_sem, gr_sem, ps_sem, pr_sem,
    gys_sem, gyr_sem, gzs_sem, gzr_sem, qs_sem, qr_sem,
):
    nz, nt, nx, rank = sizes
    replicas = nz * NY
    rep = lax.axis_index("replica")
    core = lax.axis_index("tensor")
    x = lax.axis_index("section")
    z = rep // NY
    y = rep % NY
    rows, cols = c_buf.shape
    nc = nt * NY
    steps = rows // nc

    def load(source, target):
        copy = pltpu.make_async_copy(source, target, load_sem.at[len(loads)])
        copy.start()
        loads.append(copy)

    loads = []
    load(basis_in, basis_ref)
    fold = rows // PARTS
    for k in range(PARTS):
        part = pl.ds(k * fold, fold)
        load(grads_ref.at[0, part], g_buf.at[part])
        load(error_ref.at[0, part], e_buf.at[part])

    def spot(dz=0, dy=0, dc=0, dx=0):
        return (lax.rem(z + dz, nz) * NY + lax.rem(y + dy, NY), lax.rem(core + dc, nt), lax.rem(x + dx, nx))

    cy_peers = [(dc, dy) for dc in range(nt) for dy in range(NY) if (dc, dy) != (0, 0)]
    xy_peers = [(dx, dy) for dx in range(nx) for dy in range(NY) if (dx, dy) != (0, 0)]
    cy_peers.sort(key=lambda p: (-min(p[1], NY - p[1]), -p[0]))
    xy_peers.sort(key=lambda p: -min(p[1], NY - p[1]) - min(p[0], nx - p[0]))
    z_peers = sorted(range(1, nz), key=lambda d: -min(d, nz - d))
    all_peers = [(0, 1, 0)] + [(dx, dc, dy) for dx, dy in xy_peers for dc in range(nt)]
    x_peers = (2, 1, 3)
    y_peers = (2, 1, 3)
    cx_peers = [(dx, dc) for dx in range(nx) for dc in range(nt) if (dx, dc) != (0, 0)]
    greet = {(0, dy, dc, 0) for dc, dy in cy_peers} | {(0, dy, 0, dx) for dx, dy in xy_peers}
    greet |= {(dz, 0, 0, 0) for dz in z_peers} | {(0, dy, 1, dx) for dx in range(nx) for dy in range(NY)}
    greet = sorted(greet)

    barrier = pltpu.get_barrier_semaphore()
    for dz, dy, dc, dx in greet:
        pl.semaphore_signal(barrier, inc=1, device_id=spot(dz, dy, dc, dx), device_id_type=MESH)

    sent = []

    def send(source, target, ssem, rsem, there):
        copy = pltpu.make_async_remote_copy(
            src_ref=source, dst_ref=target, send_sem=ssem, recv_sem=rsem, device_id=there, device_id_type=MESH
        )
        copy.start()
        sent.append(copy)
        return copy

    def arrive(target, ssem, rsem, there):
        pltpu.make_async_remote_copy(
            src_ref=target, dst_ref=target, send_sem=ssem, recv_sem=rsem, device_id=there, device_id_type=MESH
        ).wait_recv()

    ybit = y % 2
    zbit = z % 2

    def plan(j):
        kind = ORDER[j]
        dy = 1 - 2 * ybit if kind[1] == "+" else 2 * ybit - 1
        dz = 1 - 2 * zbit if kind[2] == "+" else 2 * zbit - 1
        to_y = spot(dy=dy + NY)
        to_z = spot(dz=dz + nz)
        if kind[0] == "y":
            return ybit, zbit, to_y, to_z
        return zbit, ybit, to_z, to_y

    def block(j, start, size):
        return pl.ds(pl.multiple_of(j * 4 * PIECE + start, PIECE), size)

    def bulk(*ops):
        for kind, j in ops:
            if kind[0] == "X":
                size = (rows - len(ORDER) * 4 * PIECE) // TAIL
                tail = pl.ds(len(ORDER) * 4 * PIECE + j * size, size)
                if kind == "X":
                    for slot, dx in enumerate(x_peers):
                        send(
                            c_buf.at[tail], moved_ref.at[nx - dx - 1, tail],
                            bs_sem.at[j, slot], br_sem.at[j, nx - dx - 1], spot(dx=dx),
                        )
                if kind == "XW":
                    for slot in range(1, nx):
                        arrive(moved_ref.at[slot - 1, tail], bs_sem.at[j, slot - 1], br_sem.at[j, slot - 1], spot(dx=slot))
                continue
            if kind == "ox":
                for slot, dx in enumerate(x_peers):
                    send(ortho.at[0, half], ortho.at[nx - dx, half], xs_sem.at[slot], xr_sem.at[nx - dx - 1], spot(dx=dx))
                continue
            if kind == "op":
                for slot in range(1, nx):
                    arrive(ortho.at[slot, half], xs_sem.at[slot - 1], xr_sem.at[slot - 1], spot(dx=slot))
                send(ortho.at[1:nx, half], ortho.at[1:nx, half], ps_sem.at[0], pr_sem.at[0], other)
                continue
            if kind == "ow":
                arrive(ortho.at[1:nx, otherhalf], ps_sem.at[0], pr_sem.at[0], other)
                continue
            low, high, first, second = plan(j)
            mine = block(j, PIECE * (2 * high + low), PIECE)
            theirs = block(j, PIECE * (2 * high + 1 - low), PIECE)
            both = block(j, 2 * PIECE * high, 2 * PIECE)
            rest = block(j, 2 * PIECE * (1 - high), 2 * PIECE)
            if kind == "x":
                for slot, dx in ((0, 1), (1, nx - 1)):
                    send(c_buf.at[mine], moved_ref.at[nx - dx - 1, mine], qs_sem.at[j, slot], qr_sem.at[j, nx - dx - 1], spot(dx=dx))
            near, far = ((0, 2), (2, 0))[j % 2]
            if kind == "r":
                arrive(moved_ref.at[near, mine], qs_sem.at[j, 0], qr_sem.at[j, near], spot(dx=near + 1))
                send(moved_ref.at[near, mine], moved_ref.at[1, mine], qs_sem.at[j, 2], qr_sem.at[j, 1], spot(dx=far + 1))
            if kind == "a":
                for slot in (far, 1):
                    arrive(moved_ref.at[slot, mine], qs_sem.at[j, slot], qr_sem.at[j, slot], spot(dx=slot + 1))
                send(moved_ref.at[:, mine], moved_ref.at[:, mine], qs_sem.at[j, 3], qr_sem.at[j, 3], first)
            if kind == "b":
                arrive(moved_ref.at[:, theirs], qs_sem.at[j, 3], qr_sem.at[j, 3], first)
                send(moved_ref.at[:, both], moved_ref.at[:, both], qs_sem.at[j, 4], qr_sem.at[j, 4], second)
            if kind == "w":
                arrive(moved_ref.at[:, rest], qs_sem.at[j, 4], qr_sem.at[j, 4], second)

    mine = core * NY + y
    other = spot(dc=1)
    half = pl.ds(core * NY, NY)
    otherhalf = pl.ds(other[1] * NY, NY)

    loads[0].wait()
    b1, b2, b3 = split3(basis_ref[...])
    pieces[0:rank, :] = b1
    pieces[rank : 2 * rank, :] = b2
    pieces[2 * rank : 3 * rank, :] = b3
    for k in range(PARTS):
        loads[1 + 2 * k].wait()
        loads[2 + 2 * k].wait()
        if k == 1:
            for source, target in (
                (weight_ref, w_buf), (momentum_ref, m_buf), (gaing_in, gaing_ref),
                (gram_in, gram_ref), (gain_in, gain_ref), (gainm_in, gainm_ref),
            ):
                load(source, target)
        part = pl.ds(k * fold, fold)
        low = dot(pieces[...], g_buf[part, :], ((1,), (1,))) + dot(pieces[...], e_buf[part, :], ((1,), (1,)))
        low = low[0:rank] + low[rank : 2 * rank] + low[2 * rank : 3 * rank]
        for i in range(fold // steps):
            left_send[k * fold // steps + i] = low[:, i * steps : (i + 1) * steps]

    pl.semaphore_wait(barrier, len(greet))

    arrivals = []
    for slot, (dc, dy) in enumerate(cy_peers):
        there = spot(dy=dy, dc=dc)
        arrivals.append(
            send(left_send.at[there[1] * NY + lax.rem(y + dy, NY)], left_recv.at[slot], ls_sem.at[slot], lr_sem.at[slot], there)
        )
    for copy in loads[1 + 2 * PARTS :]:
        copy.wait()
    for i in range(2):
        for j in range(4):
            row = i * 4 + j
            gain_y[y, row : row + 1, :] = gaing_ref[0, i : i + 1, j * LANES : (j + 1) * LANES]
    c_buf[...] = w_buf[...].astype(F32) - 0.0405 * m_buf[...]
    for slot, dy in enumerate(y_peers):
        send(gain_y.at[y], gain_y.at[y], gys_sem.at[slot], gyr_sem.at[y], spot(dy=dy))
    bulk(*PLAN[0])

    total = left_send[mine]
    for slot in range(len(cy_peers)):
        arrivals[slot].wait_recv()
        total = total + left_recv[slot]
    mid_recv[z] = total
    for slot, dz in enumerate(z_peers):
        send(mid_recv.at[z], mid_recv.at[z], ms_sem.at[slot], mr_sem.at[z], spot(dz=dz))
    for slot, dy in enumerate(y_peers):
        there = lax.rem(y + dy, NY)
        arrive(gain_y.at[there], gys_sem.at[slot], gyr_sem.at[there], spot(dy=dy))
    gain_z[z] = ((gain_y[0] + gain_y[1]) + gain_y[2]) + gain_y[3]
    bulk(*PLAN[1])
    for slot, dz in enumerate(z_peers):
        there = lax.rem(z + dz, nz)
        arrive(mid_recv.at[there], ms_sem.at[slot], mr_sem.at[there], spot(dz=dz))
    total = mid_recv[0]
    for k in range(1, nz):
        total = total + mid_recv[k]
    ortho[0, mine] = lax.dot_general(
        gram_ref[...], total * (1.0 / replicas), (((0,), (0,)), ((), ())), precision=HIGHEST, preferred_element_type=F32
    )
    for slot, (dc, dy) in enumerate(cy_peers):
        send(ortho.at[0, mine], ortho.at[0, mine], os_sem.at[slot], or_sem.at[mine], spot(dy=dy, dc=dc))
    for slot, dz in enumerate(z_peers):
        send(gain_z.at[z], gain_z.at[z], gzs_sem.at[slot], gzr_sem.at[z], spot(dz=dz))
    bulk(*PLAN[2])
    for slot, (dc, dy) in enumerate(cy_peers):
        there = spot(dy=dy, dc=dc)
        index = there[1] * NY + lax.rem(y + dy, NY)
        arrive(ortho.at[0, index], os_sem.at[slot], or_sem.at[index], there)

    for k in range(nc):
        parts = split3(ortho[0, k])
        for p in range(3):
            opieces[p * rank : (p + 1) * rank, k * steps : (k + 1) * steps] = parts[p]
    right = dot(opieces[...], g_buf[...], ((1,), (0,))) + dot(opieces[...], e_buf[...], ((1,), (0,)))
    right = right[0:rank] + right[rank : 2 * rank] + right[2 * rank : 3 * rank]
    across = cols // LANES
    for i in range(rank // SUB):
        for j in range(across):
            right_send[i * across + j] = right[i * SUB : (i + 1) * SUB, j * LANES : (j + 1) * LANES]

    place = x * NY + y
    arrivals = []
    for slot, (dx, dy) in enumerate(xy_peers):
        there = spot(dy=dy, dx=dx)
        arrivals.append(
            send(right_send.at[there[2] * NY + lax.rem(y + dy, NY)], right_recv.at[slot], rs_sem.at[slot], rr_sem.at[slot], there)
        )
    gram_own = jnp.zeros((2 * rank, 2 * rank), F32)
    for k in range(nc):
        both = opieces[0 : 2 * rank, k * steps : (k + 1) * steps]
        gram_own = gram_own + dot(both, both, ((1,), (1,)))
    pair_recv[x] = jnp.zeros((rank, LANES), F32)
    pair_recv[x, :, 0:rank] = (gram_own[0:rank, 0:rank] + gram_own[rank:, rank:]) + (
        gram_own[0:rank, rank:] + gram_own[rank:, 0:rank]
    )
    for slot, dx in enumerate(x_peers):
        send(pair_recv.at[x], pair_recv.at[x], ps_sem.at[1 + slot], pr_sem.at[1 + x], spot(dx=dx))
    bulk(*PLAN[3])
    total = right_send[place]
    for slot in range(len(xy_peers)):
        arrivals[slot].wait_recv()
        total = total + right_recv[slot]
    rmid[z] = total
    for slot, dz in enumerate(z_peers):
        send(rmid.at[z], rmid.at[z], ns_sem.at[slot], nr_sem.at[z], spot(dz=dz))
    for slot, dz in enumerate(z_peers):
        there = lax.rem(z + dz, nz)
        arrive(gain_z.at[there], gzs_sem.at[slot], gzr_sem.at[there], spot(dz=dz))
    mean = gain_z[0]
    for k in range(1, nz):
        mean = mean + gain_z[k]
    mean = mean * (1.0 / replicas)
    group = core * nx + x
    for i in range(2):
        for j in range(4):
            row, lane = i * 4 + j, slice(j * LANES, (j + 1) * LANES)
            part = mean[row : row + 1]
            new_gainm = 0.9 * gainm_ref[i : i + 1, lane] + part
            gainm_out[row : row + 1, :] = new_gainm
            gains[group, row : row + 1, :] = gain_ref[i : i + 1, lane] - 0.02 * (part + 0.9 * new_gainm)
    for slot, (dx, dc) in enumerate(cx_peers):
        send(gains.at[group], gains.at[group], gs_sem.at[slot], gr_sem.at[group], spot(dx=dx, dc=dc))
    bulk(*PLAN[4])
    for slot, dz in enumerate(z_peers):
        there = lax.rem(z + dz, nz)
        arrive(rmid.at[there], ns_sem.at[slot], nr_sem.at[there], spot(dz=dz))
    total = rmid[0]
    for k in range(1, nz):
        total = total + rmid[k]
    newb[core, place] = total * (1.0 / replicas)
    for slot, (dx, dc, dy) in enumerate(all_peers):
        send(
            newb.at[core, place], newb.at[core, place], as_sem.at[slot], ar_sem.at[core, place],
            spot(dy=dy, dx=dx, dc=dc),
        )
    bulk(*PLAN[5])

    for slot, dx in enumerate(x_peers):
        there = lax.rem(x + dx, nx)
        arrive(pair_recv.at[there], ps_sem.at[1 + slot], pr_sem.at[1 + there], spot(dx=dx))
    gsq = pair_recv[0]
    for s in range(1, nx):
        gsq = gsq + pair_recv[s]
    for slot, (dx, dc) in enumerate(cx_peers):
        there = spot(dx=dx, dc=dc)
        index = there[1] * nx + there[2]
        arrive(gains.at[index], gs_sem.at[slot], gr_sem.at[index], there)
    gains_out[...] = gains[...]
    bulk(*PLAN[6])
    for slot, (dx, dc, dy) in enumerate(all_peers):
        there = spot(dy=dy, dx=dx, dc=dc)
        index = there[2] * NY + lax.rem(y + dy, NY)
        arrive(newb.at[there[1], index], as_sem.at[slot], ar_sem.at[there[1], index], there)

    nsq = jnp.zeros((2 * rank, 2 * rank), F32)
    for c in range(nt):
        for j in range(across):
            col = jnp.concatenate([newb[c, i * across + j] for i in range(rank // SUB)], axis=0)
            parts = split3(col)
            both = jnp.concatenate(parts[0:2], axis=0)
            nsq = nsq + dot(both, both, ((1,), (1,)))
    nsq = (nsq[0:rank, 0:rank] + nsq[rank:, rank:]) + (nsq[0:rank, rank:] + nsq[rank:, 0:rank])
    nb_out[...] = newb[core]
    square = jnp.sum(gsq[:, 0:rank] * nsq)
    mean_square = square * (1.0 / (rows * cols * nt * nx))
    scale_out[...] = lax.rsqrt(jnp.full((SUB, LANES), mean_square + 1e-06, F32))
    bulk(*PLAN[7])
    ortho_out[...] = ortho[...]
    for copy in sent:
        copy.wait_send()


def apply_kernel(
    sizes, scale_ref, nb_ref, ortho_ref, gains_ref, gainm_ref, c_ref, moved_ref, g_ref, e_ref, m_ref,
    weight_out, error_out, momentum_out, gain_out, gainm_out, right, left,
):
    nz, nt, nx, rank = sizes
    step = pl.program_id(0)
    x = lax.axis_index("section")
    across = nb_ref.shape[0] // (rank // SUB)
    nc = ortho_ref.shape[1]
    order_right = (0, 1, 0)
    order_left = (0, 0, 1)

    @pl.when(step == 0)
    def _():
        for j in range(across):
            col = jnp.concatenate([nb_ref[i * across + j] for i in range(rank // SUB)], axis=0)
            parts = split3(col)
            for p in range(3):
                right[p * rank : (p + 1) * rank, j * LANES : (j + 1) * LANES] = parts[order_right[p]]
        for t in range(nt * nx):
            for i in range(2):
                for j in range(4):
                    at = (t * 4 + j) * LANES
                    gain_out[i : i + 1, at : at + LANES] = gains_ref[t, i * 4 + j : i * 4 + j + 1, :]
        for i in range(2):
            for j in range(4):
                gainm_out[i : i + 1, j * LANES : (j + 1) * LANES] = gainm_ref[i * 4 + j : i * 4 + j + 1, :]

    scale = scale_ref[0:1, 0:1]
    size = momentum_out.shape[0]
    here = pl.ds(pl.multiple_of(step * size, size), size)
    per = size // LANES

    def product(s):
        for q in range(per):
            parts = split3(ortho_ref[s, step * per + q])
            for p in range(3):
                left[p * rank : (p + 1) * rank, q * LANES : (q + 1) * LANES] = parts[order_left[p]]
        return dot(left[...], right[...], ((0,), (0,)))

    for r in range(nx):
        approx = product(r)
        base = moved_ref[r - 1, here, :] if r else c_ref[here, :]
        weight_out[lax.rem(x + r, nx)] = (base - (0.095 * scale) * approx).astype(BF16)
        if r == 0:
            error_out[0] = (g_ref[here, :].astype(F32) + e_ref[here, :].astype(F32) - approx).astype(BF16)
            momentum_out[...] = 0.9 * m_ref[here, :] + scale * approx


def on_device(weight, grads, error, momentum, basis, gram_root, gain, gain_momentum, gain_grads):
    replicas = lax.axis_size("replica")
    nt = lax.axis_size("tensor")
    nx = lax.axis_size("section")
    rows, cols = weight.shape
    rank = gram_root.shape[0]
    nz = replicas // NY
    sizes = (nz, nt, nx, rank)
    nc = nt * NY
    nxy = nx * NY
    chunk = rows // nc
    vmem = pl.BlockSpec(memory_space=pltpu.VMEM)
    hbm = pl.BlockSpec(memory_space=pl.ANY)
    dma = pltpu.SemaphoreType.DMA
    scale, newb, ortho, gains, gainm, g_here, e_here, m_here, c_here, moved = pl.pallas_call(
        functools.partial(exchange_kernel, sizes),
        out_shape=(
            jax.ShapeDtypeStruct((SUB, LANES), F32),
            jax.ShapeDtypeStruct((nxy, SUB, LANES), F32),
            jax.ShapeDtypeStruct((nx, nc, rank, chunk), F32),
            jax.ShapeDtypeStruct((nt * nx, SUB, LANES), F32),
            jax.ShapeDtypeStruct((SUB, LANES), F32),
            jax.ShapeDtypeStruct((rows, cols), BF16),
            jax.ShapeDtypeStruct((rows, cols), BF16),
            jax.ShapeDtypeStruct((rows, cols), F32),
            jax.ShapeDtypeStruct((rows, cols), F32),
            jax.ShapeDtypeStruct((nx - 1, rows, cols), F32),
        ),
        in_specs=[pl.BlockSpec(memory_space=pltpu.HBM)] * 9,
        out_specs=(vmem,) * 9 + (hbm,),
        scratch_shapes=[
            pltpu.VMEM((rows, cols), BF16),
            pltpu.VMEM((rank, cols), F32),
            pltpu.VMEM((rank, rank), F32),
            pltpu.VMEM((1, 2, cols), F32),
            pltpu.VMEM((2, cols), F32),
            pltpu.VMEM((2, cols), F32),
            pltpu.VMEM((3 * rank, cols), BF16),
            pltpu.VMEM((3 * rank, rows), BF16),
            pltpu.VMEM((nc, rank, chunk), F32),
            pltpu.VMEM((nc - 1, rank, chunk), F32),
            pltpu.VMEM((nz, rank, chunk), F32),
            pltpu.VMEM((nx, nc, rank, chunk), F32),
            pltpu.VMEM((nxy, SUB, LANES), F32),
            pltpu.VMEM((nxy - 1, SUB, LANES), F32),
            pltpu.VMEM((nz, SUB, LANES), F32),
            pltpu.VMEM((nt, nxy, SUB, LANES), F32),
            pltpu.VMEM((nt * nx, SUB, LANES), F32),
            pltpu.VMEM((NY, SUB, LANES), F32),
            pltpu.VMEM((nz, SUB, LANES), F32),
            pltpu.VMEM((nx, rank, LANES), F32),
            dma((8 + 2 * PARTS,)),
            dma((nc,)), dma((nc,)),
            dma((nz,)), dma((nz,)),
            dma((nc,)), dma((nc,)),
            dma((nx,)), dma((nx,)),
            dma((nxy,)), dma((nxy,)),
            dma((nz,)), dma((nz,)),
            dma((nt * nxy,)), dma((nt, nxy)),
            dma((TAIL, nx)), dma((TAIL, nx)),
            dma((nt * nx,)), dma((nt * nx,)),
            dma((1 + nx,)), dma((1 + nx,)),
            dma((NY,)), dma((NY,)),
            dma((nz,)), dma((nz,)),
            dma((COUNT, 5)), dma((COUNT, 5)),
        ],
        compiler_params=pltpu.CompilerParams(
            collective_id=0, has_side_effects=True, vmem_limit_bytes=24 * 1024 * 1024
        ),
    )(
        *[
            pltpu.with_memory_space_constraint(operand, pltpu.HBM)
            for operand in (grads, error, weight, momentum, basis.T, gram_root, gain_grads, gain, gain_momentum)
        ]
    )
    size = 256
    new_weight, new_error, new_momentum, new_gain, new_gainm = pl.pallas_call(
        functools.partial(apply_kernel, sizes),
        grid=(rows // size,),
        out_shape=(
            jax.ShapeDtypeStruct((nx, rows, cols), BF16),
            jax.ShapeDtypeStruct((1, rows, cols), BF16),
            jax.ShapeDtypeStruct((rows, cols), F32),
            jax.ShapeDtypeStruct((2, nt * nx * 4 * LANES), F32),
            jax.ShapeDtypeStruct((2, 4 * LANES), F32),
        ),
        in_specs=[
            vmem, vmem, vmem, vmem, vmem, vmem, vmem, vmem, vmem, vmem,
        ],
        out_specs=(
            pl.BlockSpec((nx, size, cols), lambda i: (0, i, 0)),
            pl.BlockSpec((1, size, cols), lambda i: (0, i, 0)),
            pl.BlockSpec((size, cols), lambda i: (i, 0)),
            vmem,
            vmem,
        ),
        scratch_shapes=[pltpu.VMEM((3 * rank, cols), BF16), pltpu.VMEM((3 * rank, size), BF16)],
        compiler_params=pltpu.CompilerParams(vmem_limit_bytes=24 * 1024 * 1024),
    )(scale, newb, ortho, gains, gainm, c_here, moved, g_here, e_here, m_here)
    return (new_weight.reshape(nx * rows, cols), new_error, new_momentum, new_gain, new_gainm)


def solution(mesh):
    placed = (
        P("section", "tensor"),
        P("replica", "section", "tensor"),
        P("replica", "section", "tensor"),
        P("section", "tensor"),
        P("tensor", None),
        P(),
        P(None, ("tensor", "section")),
        P(None, ("tensor", "section")),
        P("replica", None, ("tensor", "section")),
    )
    return jax.shard_map(
        on_device,
        mesh=mesh,
        in_specs=placed,
        out_specs=(
            P(None, "tensor"),
            P("replica", "section", "tensor"),
            P("section", "tensor"),
            P(),
            P(None, ("tensor", "section")),
        ),
        check_vma=False,
    )
```

```python
import functools

import jax
import jax.numpy as jnp
from jax import lax
from jax.experimental import pallas as pl
from jax.experimental.pallas import tpu as pltpu
from jax.sharding import PartitionSpec as P

MESH = pl.DeviceIdType.MESH
F32 = jnp.float32
BF16 = jnp.bfloat16
HIGHEST = lax.Precision.HIGHEST
NY = 4
LANES = 128
SUB = 8
PIECE = 16
PARTS = 2
ORDER = (
    "y++", "y--", "z+-", "z-+", "y+-", "y-+", "z++", "z--", "y++", "y--", "z+-", "z-+", "y+-", "y-+",
)
TAIL = 2
COUNT = len(ORDER)


def ops(*words):
    found = []
    for word in words:
        name = word.rstrip("0123456789")
        number = word[len(name) :]
        found.append((name, int(number) if number else 0))
    return found


PLAN = (
    ops("x0", "x1", "x2", "x3", "r0", "x4", "r1", "x5"),
    ops("r2", "x6", "r3", "x7", "a0", "a1", "r4", "x8", "r5", "x9", "a2", "a3", "r6", "x10"),
    ops("r7", "x11", "b0", "a4", "b1", "a5", "r8", "x12", "r9", "x13", "a6", "a7", "r10", "r11"),
    ops("b2", "b3", "a8", "a9", "r12", "r13", "ox", "a10", "a11"),
    ops("X0", "b4", "b5", "a12", "a13"),
    ops("op", "b6", "b7", "b8", "b9", "b10", "b11", "X1", "b12", "b13"),
    ops("ow"),
    [("w", j) for j in range(COUNT)] + [("XW", j) for j in range(TAIL)],
)


def split3(value):
    first = value.astype(BF16)
    rest = value - first.astype(F32)
    second = rest.astype(BF16)
    third = (rest - second.astype(F32)).astype(BF16)
    return first, second, third


def dot(left, right, dims):
    return lax.dot_general(left, right, (dims, ((), ())), preferred_element_type=F32)


def exchange_kernel(
    sizes,
    grads_ref, error_ref, weight_ref, momentum_ref, basis_in, gram_in, gaing_in, gain_in, gainm_in,
    scale_out, nb_out, ortho_out, gains_out, gainm_out, g_buf, e_buf, m_buf, c_buf, moved_ref,
    w_buf, basis_ref, gram_ref, gaing_ref, gain_ref, gainm_ref,
    pieces, opieces, left_send, left_recv, mid_recv, ortho, right_send, right_recv,
    rmid, newb, gains, gain_y, gain_z, pair_recv,
    load_sem, ls_sem, lr_sem, ms_sem, mr_sem, os_sem, or_sem, xs_sem, xr_sem,
    rs_sem, rr_sem, ns_sem, nr_sem, as_sem, ar_sem, bs_sem, br_sem, gs_sem, gr_sem, ps_sem, pr_sem,
    gys_sem, gyr_sem, gzs_sem, gzr_sem, qs_sem, qr_sem,
):
    nz, nt, nx, rank = sizes
    replicas = nz * NY
    rep = lax.axis_index("replica")
    core = lax.axis_index("tensor")
    x = lax.axis_index("section")
    z = rep // NY
    y = rep % NY
    rows, cols = c_buf.shape
    nc = nt * NY
    steps = rows // nc

    def load(source, target):
        copy = pltpu.make_async_copy(source, target, load_sem.at[len(loads)])
        copy.start()
        loads.append(copy)

    loads = []
    load(basis_in, basis_ref)
    fold = rows // PARTS
    for k in range(PARTS):
        part = pl.ds(k * fold, fold)
        load(grads_ref.at[0, part], g_buf.at[part])
        load(error_ref.at[0, part], e_buf.at[part])

    def spot(dz=0, dy=0, dc=0, dx=0):
        return (lax.rem(z + dz, nz) * NY + lax.rem(y + dy, NY), lax.rem(core + dc, nt), lax.rem(x + dx, nx))

    cy_peers = [(dc, dy) for dc in range(nt) for dy in range(NY) if (dc, dy) != (0, 0)]
    xy_peers = [(dx, dy) for dx in range(nx) for dy in range(NY) if (dx, dy) != (0, 0)]
    cy_peers.sort(key=lambda p: (-min(p[1], NY - p[1]), -p[0]))
    xy_peers.sort(key=lambda p: -min(p[1], NY - p[1]) - min(p[0], nx - p[0]))
    z_peers = sorted(range(1, nz), key=lambda d: -min(d, nz - d))
    all_peers = [(0, 1, 0)] + [(dx, dc, dy) for dx, dy in xy_peers for dc in range(nt)]
    x_peers = (2, 1, 3)
    y_peers = (2, 1, 3)
    cx_peers = [(dx, dc) for dx in range(nx) for dc in range(nt) if (dx, dc) != (0, 0)]
    greet = {(0, dy, dc, 0) for dc, dy in cy_peers} | {(0, dy, 0, dx) for dx, dy in xy_peers}
    greet |= {(dz, 0, 0, 0) for dz in z_peers} | {(0, dy, 1, dx) for dx in range(nx) for dy in range(NY)}
    greet = sorted(greet)

    barrier = pltpu.get_barrier_semaphore()
    for dz, dy, dc, dx in greet:
        pl.semaphore_signal(barrier, inc=1, device_id=spot(dz, dy, dc, dx), device_id_type=MESH)

    sent = []

    def send(source, target, ssem, rsem, there):
        copy = pltpu.make_async_remote_copy(
            src_ref=source, dst_ref=target, send_sem=ssem, recv_sem=rsem, device_id=there, device_id_type=MESH
        )
        copy.start()
        sent.append(copy)
        return copy

    def arrive(target, ssem, rsem, there):
        pltpu.make_async_remote_copy(
            src_ref=target, dst_ref=target, send_sem=ssem, recv_sem=rsem, device_id=there, device_id_type=MESH
        ).wait_recv()

    ybit = y % 2
    zbit = z % 2

    def plan(j):
        kind = ORDER[j]
        dy = 1 - 2 * ybit if kind[1] == "+" else 2 * ybit - 1
        dz = 1 - 2 * zbit if kind[2] == "+" else 2 * zbit - 1
        to_y = spot(dy=dy + NY)
        to_z = spot(dz=dz + nz)
        if kind[0] == "y":
            return ybit, zbit, to_y, to_z
        return zbit, ybit, to_z, to_y

    def block(j, start, size):
        return pl.ds(pl.multiple_of(j * 4 * PIECE + start, PIECE), size)

    def bulk(*ops):
        for kind, j in ops:
            if kind[0] == "X":
                size = (rows - len(ORDER) * 4 * PIECE) // TAIL
                tail = pl.ds(len(ORDER) * 4 * PIECE + j * size, size)
                if kind == "X":
                    for slot, dx in enumerate(x_peers):
                        send(
                            c_buf.at[tail], moved_ref.at[nx - dx - 1, tail],
                            bs_sem.at[j, slot], br_sem.at[j, nx - dx - 1], spot(dx=dx),
                        )
                if kind == "XW":
                    for slot in range(1, nx):
                        arrive(moved_ref.at[slot - 1, tail], bs_sem.at[j, slot - 1], br_sem.at[j, slot - 1], spot(dx=slot))
                continue
            if kind == "ox":
                for slot, dx in enumerate(x_peers):
                    send(ortho.at[0, half], ortho.at[nx - dx, half], xs_sem.at[slot], xr_sem.at[nx - dx - 1], spot(dx=dx))
                continue
            if kind == "op":
                for slot in range(1, nx):
                    arrive(ortho.at[slot, half], xs_sem.at[slot - 1], xr_sem.at[slot - 1], spot(dx=slot))
                send(ortho.at[1:nx, half], ortho.at[1:nx, half], ps_sem.at[0], pr_sem.at[0], other)
                continue
            if kind == "ow":
                arrive(ortho.at[1:nx, otherhalf], ps_sem.at[0], pr_sem.at[0], other)
                continue
            low, high, first, second = plan(j)
            mine = block(j, PIECE * (2 * high + low), PIECE)
            theirs = block(j, PIECE * (2 * high + 1 - low), PIECE)
            both = block(j, 2 * PIECE * high, 2 * PIECE)
            rest = block(j, 2 * PIECE * (1 - high), 2 * PIECE)
            if kind == "x":
                for slot, dx in ((0, 1), (1, nx - 1)):
                    send(c_buf.at[mine], moved_ref.at[nx - dx - 1, mine], qs_sem.at[j, slot], qr_sem.at[j, nx - dx - 1], spot(dx=dx))
            near, far = ((0, 2), (2, 0))[j % 2]
            if kind == "r":
                arrive(moved_ref.at[near, mine], qs_sem.at[j, 0], qr_sem.at[j, near], spot(dx=near + 1))
                send(moved_ref.at[near, mine], moved_ref.at[1, mine], qs_sem.at[j, 2], qr_sem.at[j, 1], spot(dx=far + 1))
            if kind == "a":
                for slot in (far, 1):
                    arrive(moved_ref.at[slot, mine], qs_sem.at[j, slot], qr_sem.at[j, slot], spot(dx=slot + 1))
                send(moved_ref.at[:, mine], moved_ref.at[:, mine], qs_sem.at[j, 3], qr_sem.at[j, 3], first)
            if kind == "b":
                arrive(moved_ref.at[:, theirs], qs_sem.at[j, 3], qr_sem.at[j, 3], first)
                send(moved_ref.at[:, both], moved_ref.at[:, both], qs_sem.at[j, 4], qr_sem.at[j, 4], second)
            if kind == "w":
                arrive(moved_ref.at[:, rest], qs_sem.at[j, 4], qr_sem.at[j, 4], second)

    mine = core * NY + y
    other = spot(dc=1)
    half = pl.ds(core * NY, NY)
    otherhalf = pl.ds(other[1] * NY, NY)

    loads[0].wait()
    b1, b2, b3 = split3(basis_ref[...])
    pieces[0:rank, :] = b1
    pieces[rank : 2 * rank, :] = b2
    pieces[2 * rank : 3 * rank, :] = b3
    for k in range(PARTS):
        loads[1 + 2 * k].wait()
        loads[2 + 2 * k].wait()
        if k == 0:
            for source, target in (
                (weight_ref, w_buf), (momentum_ref, m_buf), (gaing_in, gaing_ref),
                (gram_in, gram_ref), (gain_in, gain_ref), (gainm_in, gainm_ref),
            ):
                load(source, target)
        part = pl.ds(k * fold, fold)
        low = dot(pieces[...], g_buf[part, :], ((1,), (1,))) + dot(pieces[...], e_buf[part, :], ((1,), (1,)))
        low = low[0:rank] + low[rank : 2 * rank] + low[2 * rank : 3 * rank]
        for i in range(fold // steps):
            left_send[k * fold // steps + i] = low[:, i * steps : (i + 1) * steps]

    for copy in loads[1 + 2 * PARTS :]:
        copy.wait()
    for i in range(2):
        for j in range(4):
            row = i * 4 + j
            gain_y[y, row : row + 1, :] = gaing_ref[0, i : i + 1, j * LANES : (j + 1) * LANES]
    c_buf[...] = w_buf[...].astype(F32) - 0.0405 * m_buf[...]

    pl.semaphore_wait(barrier, len(greet))

    arrivals = []
    for slot, (dc, dy) in enumerate(cy_peers):
        there = spot(dy=dy, dc=dc)
        arrivals.append(
            send(left_send.at[there[1] * NY + lax.rem(y + dy, NY)], left_recv.at[slot], ls_sem.at[slot], lr_sem.at[slot], there)
        )
    for slot, dy in enumerate(y_peers):
        send(gain_y.at[y], gain_y.at[y], gys_sem.at[slot], gyr_sem.at[y], spot(dy=dy))
    bulk(*PLAN[0])

    total = left_send[mine]
    for slot in range(len(cy_peers)):
        arrivals[slot].wait_recv()
        total = total + left_recv[slot]
    mid_recv[z] = total
    for slot, dz in enumerate(z_peers):
        send(mid_recv.at[z], mid_recv.at[z], ms_sem.at[slot], mr_sem.at[z], spot(dz=dz))
    for slot, dy in enumerate(y_peers):
        there = lax.rem(y + dy, NY)
        arrive(gain_y.at[there], gys_sem.at[slot], gyr_sem.at[there], spot(dy=dy))
    gain_z[z] = ((gain_y[0] + gain_y[1]) + gain_y[2]) + gain_y[3]
    bulk(*PLAN[1])
    for slot, dz in enumerate(z_peers):
        there = lax.rem(z + dz, nz)
        arrive(mid_recv.at[there], ms_sem.at[slot], mr_sem.at[there], spot(dz=dz))
    total = mid_recv[0]
    for k in range(1, nz):
        total = total + mid_recv[k]
    ortho[0, mine] = lax.dot_general(
        gram_ref[...], total * (1.0 / replicas), (((0,), (0,)), ((), ())), precision=HIGHEST, preferred_element_type=F32
    )
    for slot, (dc, dy) in enumerate(cy_peers):
        send(ortho.at[0, mine], ortho.at[0, mine], os_sem.at[slot], or_sem.at[mine], spot(dy=dy, dc=dc))
    for slot, dz in enumerate(z_peers):
        send(gain_z.at[z], gain_z.at[z], gzs_sem.at[slot], gzr_sem.at[z], spot(dz=dz))
    bulk(*PLAN[2])
    for slot, (dc, dy) in enumerate(cy_peers):
        there = spot(dy=dy, dc=dc)
        index = there[1] * NY + lax.rem(y + dy, NY)
        arrive(ortho.at[0, index], os_sem.at[slot], or_sem.at[index], there)

    for k in range(nc):
        parts = split3(ortho[0, k])
        for p in range(3):
            opieces[p * rank : (p + 1) * rank, k * steps : (k + 1) * steps] = parts[p]
    right = dot(opieces[...], g_buf[...], ((1,), (0,))) + dot(opieces[...], e_buf[...], ((1,), (0,)))
    right = right[0:rank] + right[rank : 2 * rank] + right[2 * rank : 3 * rank]
    across = cols // LANES
    for i in range(rank // SUB):
        for j in range(across):
            right_send[i * across + j] = right[i * SUB : (i + 1) * SUB, j * LANES : (j + 1) * LANES]

    place = x * NY + y
    arrivals = []
    for slot, (dx, dy) in enumerate(xy_peers):
        there = spot(dy=dy, dx=dx)
        arrivals.append(
            send(right_send.at[there[2] * NY + lax.rem(y + dy, NY)], right_recv.at[slot], rs_sem.at[slot], rr_sem.at[slot], there)
        )
    gram_own = jnp.zeros((2 * rank, 2 * rank), F32)
    for k in range(nc):
        both = opieces[0 : 2 * rank, k * steps : (k + 1) * steps]
        gram_own = gram_own + dot(both, both, ((1,), (1,)))
    pair_recv[x] = jnp.zeros((rank, LANES), F32)
    pair_recv[x, :, 0:rank] = (gram_own[0:rank, 0:rank] + gram_own[rank:, rank:]) + (
        gram_own[0:rank, rank:] + gram_own[rank:, 0:rank]
    )
    for slot, dx in enumerate(x_peers):
        send(pair_recv.at[x], pair_recv.at[x], ps_sem.at[1 + slot], pr_sem.at[1 + x], spot(dx=dx))
    bulk(*PLAN[3])
    total = right_send[place]
    for slot in range(len(xy_peers)):
        arrivals[slot].wait_recv()
        total = total + right_recv[slot]
    rmid[z] = total
    for slot, dz in enumerate(z_peers):
        send(rmid.at[z], rmid.at[z], ns_sem.at[slot], nr_sem.at[z], spot(dz=dz))
    for slot, dz in enumerate(z_peers):
        there = lax.rem(z + dz, nz)
        arrive(gain_z.at[there], gzs_sem.at[slot], gzr_sem.at[there], spot(dz=dz))
    mean = gain_z[0]
    for k in range(1, nz):
        mean = mean + gain_z[k]
    mean = mean * (1.0 / replicas)
    group = core * nx + x
    for i in range(2):
        for j in range(4):
            row, lane = i * 4 + j, slice(j * LANES, (j + 1) * LANES)
            part = mean[row : row + 1]
            new_gainm = 0.9 * gainm_ref[i : i + 1, lane] + part
            gainm_out[row : row + 1, :] = new_gainm
            gains[group, row : row + 1, :] = gain_ref[i : i + 1, lane] - 0.02 * (part + 0.9 * new_gainm)
    for slot, (dx, dc) in enumerate(cx_peers):
        send(gains.at[group], gains.at[group], gs_sem.at[slot], gr_sem.at[group], spot(dx=dx, dc=dc))
    bulk(*PLAN[4])
    for slot, dz in enumerate(z_peers):
        there = lax.rem(z + dz, nz)
        arrive(rmid.at[there], ns_sem.at[slot], nr_sem.at[there], spot(dz=dz))
    total = rmid[0]
    for k in range(1, nz):
        total = total + rmid[k]
    newb[core, place] = total * (1.0 / replicas)
    for slot, (dx, dc, dy) in enumerate(all_peers):
        send(
            newb.at[core, place], newb.at[core, place], as_sem.at[slot], ar_sem.at[core, place],
            spot(dy=dy, dx=dx, dc=dc),
        )
    bulk(*PLAN[5])

    for slot, dx in enumerate(x_peers):
        there = lax.rem(x + dx, nx)
        arrive(pair_recv.at[there], ps_sem.at[1 + slot], pr_sem.at[1 + there], spot(dx=dx))
    gsq = pair_recv[0]
    for s in range(1, nx):
        gsq = gsq + pair_recv[s]
    for slot, (dx, dc) in enumerate(cx_peers):
        there = spot(dx=dx, dc=dc)
        index = there[1] * nx + there[2]
        arrive(gains.at[index], gs_sem.at[slot], gr_sem.at[index], there)
    gains_out[...] = gains[...]
    bulk(*PLAN[6])
    for slot, (dx, dc, dy) in enumerate(all_peers):
        there = spot(dy=dy, dx=dx, dc=dc)
        index = there[2] * NY + lax.rem(y + dy, NY)
        arrive(newb.at[there[1], index], as_sem.at[slot], ar_sem.at[there[1], index], there)

    nsq = jnp.zeros((2 * rank, 2 * rank), F32)
    for c in range(nt):
        for j in range(across):
            col = jnp.concatenate([newb[c, i * across + j] for i in range(rank // SUB)], axis=0)
            parts = split3(col)
            both = jnp.concatenate(parts[0:2], axis=0)
            nsq = nsq + dot(both, both, ((1,), (1,)))
    nsq = (nsq[0:rank, 0:rank] + nsq[rank:, rank:]) + (nsq[0:rank, rank:] + nsq[rank:, 0:rank])
    nb_out[...] = newb[core]
    square = jnp.sum(gsq[:, 0:rank] * nsq)
    mean_square = square * (1.0 / (rows * cols * nt * nx))
    scale_out[...] = lax.rsqrt(jnp.full((SUB, LANES), mean_square + 1e-06, F32))
    bulk(*PLAN[7])
    ortho_out[...] = ortho[...]
    for copy in sent:
        copy.wait_send()


def apply_kernel(
    sizes, scale_ref, nb_ref, ortho_ref, gains_ref, gainm_ref, c_ref, moved_ref, g_ref, e_ref, m_ref,
    weight_out, error_out, momentum_out, gain_out, gainm_out, right, left,
):
    nz, nt, nx, rank = sizes
    step = pl.program_id(0)
    x = lax.axis_index("section")
    across = nb_ref.shape[0] // (rank // SUB)
    nc = ortho_ref.shape[1]
    order_right = (0, 1, 0)
    order_left = (0, 0, 1)

    @pl.when(step == 0)
    def _():
        for j in range(across):
            col = jnp.concatenate([nb_ref[i * across + j] for i in range(rank // SUB)], axis=0)
            parts = split3(col)
            for p in range(3):
                right[p * rank : (p + 1) * rank, j * LANES : (j + 1) * LANES] = parts[order_right[p]]
        for t in range(nt * nx):
            for i in range(2):
                for j in range(4):
                    at = (t * 4 + j) * LANES
                    gain_out[i : i + 1, at : at + LANES] = gains_ref[t, i * 4 + j : i * 4 + j + 1, :]
        for i in range(2):
            for j in range(4):
                gainm_out[i : i + 1, j * LANES : (j + 1) * LANES] = gainm_ref[i * 4 + j : i * 4 + j + 1, :]

    scale = scale_ref[0:1, 0:1]
    size = momentum_out.shape[0]
    here = pl.ds(pl.multiple_of(step * size, size), size)
    per = size // LANES

    def product(s):
        for q in range(per):
            parts = split3(ortho_ref[s, step * per + q])
            for p in range(3):
                left[p * rank : (p + 1) * rank, q * LANES : (q + 1) * LANES] = parts[order_left[p]]
        return dot(left[...], right[...], ((0,), (0,)))

    for r in range(nx):
        approx = product(r)
        base = moved_ref[r - 1, here, :] if r else c_ref[here, :]
        weight_out[lax.rem(x + r, nx)] = (base - (0.095 * scale) * approx).astype(BF16)
        if r == 0:
            error_out[0] = (g_ref[here, :].astype(F32) + e_ref[here, :].astype(F32) - approx).astype(BF16)
            momentum_out[...] = 0.9 * m_ref[here, :] + scale * approx


def on_device(weight, grads, error, momentum, basis, gram_root, gain, gain_momentum, gain_grads):
    replicas = lax.axis_size("replica")
    nt = lax.axis_size("tensor")
    nx = lax.axis_size("section")
    rows, cols = weight.shape
    rank = gram_root.shape[0]
    nz = replicas // NY
    sizes = (nz, nt, nx, rank)
    nc = nt * NY
    nxy = nx * NY
    chunk = rows // nc
    vmem = pl.BlockSpec(memory_space=pltpu.VMEM)
    hbm = pl.BlockSpec(memory_space=pl.ANY)
    dma = pltpu.SemaphoreType.DMA
    scale, newb, ortho, gains, gainm, g_here, e_here, m_here, c_here, moved = pl.pallas_call(
        functools.partial(exchange_kernel, sizes),
        out_shape=(
            jax.ShapeDtypeStruct((SUB, LANES), F32),
            jax.ShapeDtypeStruct((nxy, SUB, LANES), F32),
            jax.ShapeDtypeStruct((nx, nc, rank, chunk), F32),
            jax.ShapeDtypeStruct((nt * nx, SUB, LANES), F32),
            jax.ShapeDtypeStruct((SUB, LANES), F32),
            jax.ShapeDtypeStruct((rows, cols), BF16),
            jax.ShapeDtypeStruct((rows, cols), BF16),
            jax.ShapeDtypeStruct((rows, cols), F32),
            jax.ShapeDtypeStruct((rows, cols), F32),
            jax.ShapeDtypeStruct((nx - 1, rows, cols), F32),
        ),
        in_specs=[pl.BlockSpec(memory_space=pltpu.HBM)] * 9,
        out_specs=(vmem,) * 9 + (hbm,),
        scratch_shapes=[
            pltpu.VMEM((rows, cols), BF16),
            pltpu.VMEM((rank, cols), F32),
            pltpu.VMEM((rank, rank), F32),
            pltpu.VMEM((1, 2, cols), F32),
            pltpu.VMEM((2, cols), F32),
            pltpu.VMEM((2, cols), F32),
            pltpu.VMEM((3 * rank, cols), BF16),
            pltpu.VMEM((3 * rank, rows), BF16),
            pltpu.VMEM((nc, rank, chunk), F32),
            pltpu.VMEM((nc - 1, rank, chunk), F32),
            pltpu.VMEM((nz, rank, chunk), F32),
            pltpu.VMEM((nx, nc, rank, chunk), F32),
            pltpu.VMEM((nxy, SUB, LANES), F32),
            pltpu.VMEM((nxy - 1, SUB, LANES), F32),
            pltpu.VMEM((nz, SUB, LANES), F32),
            pltpu.VMEM((nt, nxy, SUB, LANES), F32),
            pltpu.VMEM((nt * nx, SUB, LANES), F32),
            pltpu.VMEM((NY, SUB, LANES), F32),
            pltpu.VMEM((nz, SUB, LANES), F32),
            pltpu.VMEM((nx, rank, LANES), F32),
            dma((8 + 2 * PARTS,)),
            dma((nc,)), dma((nc,)),
            dma((nz,)), dma((nz,)),
            dma((nc,)), dma((nc,)),
            dma((nx,)), dma((nx,)),
            dma((nxy,)), dma((nxy,)),
            dma((nz,)), dma((nz,)),
            dma((nt * nxy,)), dma((nt, nxy)),
            dma((TAIL, nx)), dma((TAIL, nx)),
            dma((nt * nx,)), dma((nt * nx,)),
            dma((1 + nx,)), dma((1 + nx,)),
            dma((NY,)), dma((NY,)),
            dma((nz,)), dma((nz,)),
            dma((COUNT, 5)), dma((COUNT, 5)),
        ],
        compiler_params=pltpu.CompilerParams(
            collective_id=0, has_side_effects=True, vmem_limit_bytes=24 * 1024 * 1024
        ),
    )(
        *[
            pltpu.with_memory_space_constraint(operand, pltpu.HBM)
            for operand in (grads, error, weight, momentum, basis.T, gram_root, gain_grads, gain, gain_momentum)
        ]
    )
    size = 256
    new_weight, new_error, new_momentum, new_gain, new_gainm = pl.pallas_call(
        functools.partial(apply_kernel, sizes),
        grid=(rows // size,),
        out_shape=(
            jax.ShapeDtypeStruct((nx, rows, cols), BF16),
            jax.ShapeDtypeStruct((1, rows, cols), BF16),
            jax.ShapeDtypeStruct((rows, cols), F32),
            jax.ShapeDtypeStruct((2, nt * nx * 4 * LANES), F32),
            jax.ShapeDtypeStruct((2, 4 * LANES), F32),
        ),
        in_specs=[
            vmem, vmem, vmem, vmem, vmem, vmem, vmem, vmem, vmem, vmem,
        ],
        out_specs=(
            pl.BlockSpec((nx, size, cols), lambda i: (0, i, 0)),
            pl.BlockSpec((1, size, cols), lambda i: (0, i, 0)),
            pl.BlockSpec((size, cols), lambda i: (i, 0)),
            vmem,
            vmem,
        ),
        scratch_shapes=[pltpu.VMEM((3 * rank, cols), BF16), pltpu.VMEM((3 * rank, size), BF16)],
        compiler_params=pltpu.CompilerParams(vmem_limit_bytes=24 * 1024 * 1024),
    )(scale, newb, ortho, gains, gainm, c_here, moved, g_here, e_here, m_here)
    return (new_weight.reshape(nx * rows, cols), new_error, new_momentum, new_gain, new_gainm)


def solution(mesh):
    placed = (
        P("section", "tensor"),
        P("replica", "section", "tensor"),
        P("replica", "section", "tensor"),
        P("section", "tensor"),
        P("tensor", None),
        P(),
        P(None, ("tensor", "section")),
        P(None, ("tensor", "section")),
        P("replica", None, ("tensor", "section")),
    )
    return jax.shard_map(
        on_device,
        mesh=mesh,
        in_specs=placed,
        out_specs=(
            P(None, "tensor"),
            P("replica", "section", "tensor"),
            P("section", "tensor"),
            P(),
            P(None, ("tensor", "section")),
        ),
        check_vma=False,
    )
```
